1024 devices in a mesh: dp: 16 (over y, x), seq: 64 (over z, core).
Axes of the slice: x: 4, y: 4, z: 32, core: 2. Of those that a mesh axis runs over, the one named last changes fastest.
Arguments:
- qkvu: bfloat16 [131072, 4096], P(('dp', 'seq')), may hold values from -6 to 6
- w_out: bfloat16 [1024, 1024], replicated, may hold values from -0.1875 to 0.1875
- head_coef: bfloat16 [131072, 256], P(('dp', 'seq')), may hold values from -0.375 to 0.375
- item_table: bfloat16 [32768, 1024], P('seq'), may hold values from -6 to 6
- neg_ids: int32 [256], P('seq'), may hold values from 0 to 511
- send_order: int32 [1024, 128], P(('dp', 'seq')), may hold values from 0 to 127, each once within a row
- recv_order: int32 [1024, 128], P(('dp', 'seq')), may hold values from 0 to 127, each once within a row
- tile_len: int32 [16, 64], P('dp'), may hold values from 1 to 128, 2730 in all within a row
Outputs:
- layer_out: bfloat16 [131072, 1024], P(('dp', 'seq'))
- d_qkvu: bfloat16 [131072, 4096], P(('dp', 'seq'))
- d_w_out: float32 [1024, 1024], P('seq', 'dp')
The draws below stay inside these ranges and needn't reach their ends.
Inputs may be any that keep to these rules, and one draw needn't show every extreme that they name: Each row of send_order and of recv_order names every number once. `recv_order`: each row names every number once. `tile_len`: in each data group the lengths sum to 2730.
All inputs are finite; a program needn't handle non-finite values.
Results may differ from the reference program's by a relative error of at most 0.014.
Values may be sent and summed in bfloat16 or wider, within the bound.
A program may use at most 32 MiB of HBM per device.

```python
import math
import jax
import jax.numpy as jnp
import numpy as np
from jax import lax

D = 1024
HEADS = 8
TILE = 128
SPAN = 3
NEG = 4
ITEMS_DEV = 512
NEGS = 256
ITEMS = 32768
TOKENS = 131072
N_DP = 16
N_SEQ = 64


def plant(result, rng, least, top_value):
    longest = result.shape.index(max(result.shape))
    spots = []
    for shift in (0, 1):
        where = [jax.random.randint(jax.random.fold_in(rng, axis), (), 0, length) for axis, length in enumerate(result.shape)]
        where[longest] = (where[longest] + shift) % result.shape[longest]
        spots.append(tuple(where))
    return result.at[spots[0]].set(least).at[spots[1]].set(top_value)


def block_levels(key, extent, pieces, smallest, top_value):
    level, own = 1.0, jax.random.fold_in(key, 6)
    for position, blocks in pieces:
        steps = jnp.exp(jax.random.uniform(jax.random.fold_in(own, position), (blocks,), jnp.float32, smallest / len(pieces), top_value / len(pieces)))
        level = level * jnp.repeat(steps, extent[position] // blocks).reshape([-1 if axis == position else 1 for axis in range(len(extent))])
    return level


def length_profile(number_of, total, limit, lean):
    portions = [(1 << 20) // math.isqrt(rank ** lean) + 1 for rank in range(2, number_of + 1)]
    surplus, counts = total - limit - (number_of - 1), [1] * (number_of - 1)
    while surplus > 0:
        free = [i for i in range(number_of - 1) if counts[i] < limit]
        whole, left = sum([portions[i] for i in free]), surplus
        for i in free:
            extra = min(limit - counts[i], max(1, left * portions[i] // whole), surplus)
            counts[i] = counts[i] + extra
            surplus = surplus - extra
    return np.array([limit] + counts)


def ragged_sizes(key, number_of, total, most, slope):
    if number_of == 2:
        one = jax.random.randint(key, (), max(1, total - most), min(most, total - 1) + 1)
        return jnp.stack([one, total - one])
    tallies = jnp.asarray(length_profile(number_of, total, most, slope), jnp.int32)
    couples = (number_of - 1) // 2
    giver, taker = tallies[1:1 + 2 * couples:2], tallies[2:2 + 2 * couples:2]
    margin = jnp.minimum(giver - 1, most - taker)
    passed = jax.random.randint(jax.random.fold_in(key, 1), (couples,), 0, 1 << 20) % (margin + 1)
    tallies = tallies.at[1:1 + 2 * couples:2].set(giver - passed).at[2:2 + 2 * couples:2].set(taker + passed)
    return tallies[jax.random.permutation(jax.random.fold_in(key, 2), number_of)]


def gaussian(rng, shape, deviation, reach, pieces=(), held_as=jnp.bfloat16):
    array = jax.random.normal(rng, shape, jnp.float32) * deviation
    if len(pieces) > 0:
        array = block_levels(rng, shape, pieces, -0.22, 0.18) * array
    return jnp.clip(array, min=-reach, max=reach).astype(held_as)


def setup_inputs(seed: int = 0) -> dict:
    key_of = jax.random.split(jax.random.key(seed), 9)
    return {
        "qkvu": gaussian(key_of[0], (TOKENS, 4 * D), 1.0, 6.0, ((0, 1024),)),
        "w_out": gaussian(key_of[1], (D, D), D ** -0.5, 0.1875),
        "head_coef": gaussian(key_of[2], (TOKENS, NEGS), NEGS ** -0.5, 0.375, ((0, 1024),)),
        "item_table": gaussian(key_of[3], (ITEMS, D), 1.0, 6.0, ((0, 64),)),
        "neg_ids": plant(jax.random.randint(key_of[4], (NEGS,), 0, ITEMS_DEV), jax.random.fold_in(key_of[4], 1), 0, ITEMS_DEV - 1).astype(jnp.int32),
        "send_order": jax.vmap(lambda own: jax.random.permutation(own, TILE))(jax.random.split(key_of[5], (N_DP * N_SEQ))).reshape((N_DP * N_SEQ, TILE)).astype(jnp.int32),
        "recv_order": jax.vmap(lambda own: jax.random.permutation(own, TILE))(jax.random.split(key_of[6], (N_DP * N_SEQ))).reshape((N_DP * N_SEQ, TILE)).astype(jnp.int32),
        "tile_len": jax.vmap(lambda own: ragged_sizes(own, N_SEQ, N_SEQ * TILE // 3, TILE, 2))(jax.random.split(key_of[7], N_DP)).reshape((N_DP, N_SEQ)).astype(jnp.int32),
    }


eps = 1e-05

def silu_grad(values):
    sigmoid_val = jax.nn.sigmoid(values)
    return sigmoid_val * (1.0 + values * (1.0 - sigmoid_val))

def split_rows(rows_in, width):
    count = rows_in.shape[0]
    head_dim = width // HEADS
    u_part = rows_in[:, :width].astype(jnp.float32)
    value_rows = rows_in[:, width:2 * width].astype(jnp.float32).reshape(count, HEADS, head_dim)
    query_rows = rows_in[:, 2 * width:3 * width].astype(jnp.float32).reshape(count, HEADS, head_dim)
    key_rows = rows_in[:, 3 * width:].astype(jnp.float32).reshape(count, HEADS, head_dim)
    return (u_part, value_rows, query_rows, key_rows)

def pair_mask(count, len_p, len_q, causal):
    positions = jnp.arange(count, dtype=jnp.int32)
    live = (positions[:, None] < len_p) & (positions[None, :] < len_q)
    if causal:
        live = live & (positions[None, :] <= positions[:, None])
    return jnp.where(live, 1.0, 0.0).astype(jnp.float32)

def history_step(bal, coef, lens, neg_rows, w_out):
    tiles = bal.shape[0]
    count = bal.shape[1]
    width = w_out.shape[0]
    head_dim = width // HEADS
    score_scale = 1.0 / math.sqrt(head_dim)
    positions = jnp.arange(count, dtype=jnp.int32)
    split = [split_rows(bal[i], width) for i in range(tiles)]
    sampled = jnp.zeros((width, coef.shape[2]), jnp.float32)
    key_grads = [jnp.zeros((count, HEADS, head_dim), jnp.float32) for i in range(tiles)]
    value_grads = [jnp.zeros((count, HEADS, head_dim), jnp.float32) for i in range(tiles)]
    outputs = []
    u_grads = []
    query_grads = []
    for i in range(tiles):
        u_part, value_i, query_i, key_i = split[i]
        window = list(range(max(0, i - SPAN + 1), i + 1))
        attended = jnp.zeros((count, HEADS, head_dim), jnp.float32)
        saved = []
        for j in window:
            mask = pair_mask(count, lens[i], lens[j], j == i)
            scores = jnp.einsum('phd,qhd->hpq', query_i, split[j][3]) * score_scale
            weights = (jax.nn.silu(scores) * mask[None] / count).astype(jnp.bfloat16)
            attended = attended + jnp.einsum('hpq,qhd->phd', weights.astype(jnp.float32), split[j][1])
            saved.append((j, mask, scores, weights))
        attended = attended.reshape(count, width)
        row_mean = lax.optimization_barrier(jnp.mean(attended, axis=1, keepdims=True))
        centered = attended - row_mean
        variance = lax.optimization_barrier(jnp.mean(centered * centered, axis=1, keepdims=True))
        inv_std = lax.rsqrt(variance + eps)
        normed = centered * inv_std
        mixed_rows = (normed * u_part).astype(jnp.bfloat16)
        outputs.append(jnp.dot(mixed_rows, w_out, preferred_element_type=jnp.float32).astype(jnp.bfloat16))
        live_col = jnp.where(positions < lens[i], 1.0, 0.0).astype(jnp.float32)[:, None]
        coef_live = (coef[i] * live_col).astype(jnp.bfloat16)
        head_grad = jnp.dot(coef_live, neg_rows, preferred_element_type=jnp.float32).astype(jnp.bfloat16)
        sampled = sampled + lax.dot_general(mixed_rows, coef_live, (((0,), (0,)), ((), ())), preferred_element_type=jnp.float32)
        d_mixed = lax.dot_general(head_grad, w_out, (((1,), (1,)), ((), ())), preferred_element_type=jnp.float32)
        u_grads.append(d_mixed * normed)
        d_normed = d_mixed * u_part
        d_att = (d_normed - lax.optimization_barrier(jnp.mean(d_normed, axis=1, keepdims=True)) - normed * lax.optimization_barrier(jnp.mean(d_normed * normed, axis=1, keepdims=True))) * inv_std
        d_att = d_att.astype(jnp.bfloat16).astype(jnp.float32).reshape(count, HEADS, head_dim)
        d_query = jnp.zeros((count, HEADS, head_dim), jnp.float32)
        for j, mask, scores, weights in saved:
            d_weights = jnp.einsum('phd,qhd->hpq', d_att, split[j][1])
            d_scores = (d_weights * mask[None] / count * silu_grad(scores) * score_scale).astype(jnp.bfloat16).astype(jnp.float32)
            d_query = d_query + jnp.einsum('hpq,qhd->phd', d_scores, split[j][3])
            part_keys = jnp.einsum('hpq,phd->qhd', d_scores, query_i)
            part_values = jnp.einsum('hpq,phd->qhd', weights.astype(jnp.float32), d_att)
            if j < i:
                part_keys = part_keys.astype(jnp.bfloat16).astype(jnp.float32)
                part_values = part_values.astype(jnp.bfloat16).astype(jnp.float32)
            key_grads[j] = key_grads[j] + part_keys
            value_grads[j] = value_grads[j] + part_values
        query_grads.append(d_query.reshape(count, width))
    grads = []
    for i in range(tiles):
        grads.append(jnp.concatenate([u_grads[i], value_grads[i].reshape(count, width), query_grads[i], key_grads[i].reshape(count, width)], axis=1).astype(jnp.bfloat16))
    return (jnp.stack(outputs), jnp.stack(grads), sampled)

def place_rows(values, indices):
    return jnp.zeros_like(values).at[indices].set(values)

def reference(qkvu, w_out, head_coef, item_table, neg_ids, send_order, recv_order, tile_len):
    groups = N_DP
    peer_count = N_SEQ
    slot_cap = TILE // N_SEQ
    full_width = 4 * D
    home_rows = qkvu.reshape(groups, peer_count, TILE, full_width)
    send_list = send_order.reshape(groups, peer_count, TILE).astype(jnp.int32)
    recv_list = recv_order.reshape(groups, peer_count, TILE).astype(jnp.int32)
    sent_rows = jnp.take_along_axis(home_rows, send_list[..., None], axis=2)
    sent_rows = sent_rows.reshape(groups, peer_count, peer_count, slot_cap, full_width)
    received = jnp.swapaxes(sent_rows, 1, 2).reshape(groups, peer_count, TILE, full_width)
    balanced = jnp.take_along_axis(received, recv_list[..., None], axis=2)
    table_shards = item_table.reshape(peer_count, ITEMS_DEV, D)
    id_shards = neg_ids.reshape(peer_count, NEG).astype(jnp.int32)
    neg_rows = jnp.take_along_axis(table_shards, id_shards[..., None], axis=1).reshape(peer_count * NEG, D)
    device_count = groups * peer_count
    hist_coef = head_coef.reshape(groups, peer_count, TILE, NEG * peer_count)
    hist_len = tile_len.reshape(groups, peer_count).astype(jnp.int32)

    def per_history(running_sum, inputs):
        bal_rows, coef_rows, lens = inputs
        outs, grads, sampled = history_step(bal_rows, coef_rows, lens, neg_rows, w_out)
        return (running_sum + sampled, (outs, grads))
    sampled_total, (outputs, grads_bal) = lax.scan(per_history, jnp.zeros((D, NEG * peer_count), jnp.float32), (balanced, hist_coef, hist_len))
    d_w_out = jnp.dot(sampled_total, neg_rows.astype(jnp.float32), precision=lax.Precision.HIGHEST)
    grads_bal = grads_bal.reshape(device_count, TILE, full_width)
    slot_grads = jax.vmap(place_rows)(grads_bal, recv_list.reshape(device_count, TILE))
    slot_grads = slot_grads.reshape(groups, peer_count, peer_count, slot_cap, full_width)
    slot_grads = jnp.swapaxes(slot_grads, 1, 2).reshape(device_count, TILE, full_width)
    d_home = jax.vmap(place_rows)(slot_grads, send_list.reshape(device_count, TILE))
    return (outputs.reshape(TILE * device_count, D), d_home.reshape(TILE * device_count, full_width), d_w_out)
```

```python
import functools
import math

import jax
import jax.numpy as jnp
from jax import lax
from jax.experimental import pallas as pl
from jax.experimental.pallas import tpu as pltpu
from jax.sharding import PartitionSpec as P

HEADS = 8
SPAN = 3
CH = 256
eps = 1e-05
BF = jnp.bfloat16
F32 = jnp.float32
MESH = pl.DeviceIdType.MESH


def iota(shape, dim):
    return lax.broadcasted_iota(jnp.int32, shape, dim)


def mm(a, b):
    return jnp.dot(a, b, preferred_element_type=F32)


def mm_nt(a, b):
    return lax.dot_general(a, b, (((1,), (1,)), ((), ())), preferred_element_type=F32)


def mm_tn(a, b):
    return lax.dot_general(a, b, (((0,), (0,)), ((), ())), preferred_element_type=F32)


def kernel(
    n_dp, n_seq,
    ids_ref, len_ref, qkvu_ref, w_ref, coef_ref, table_ref, send_ref, recv_ref,
    out_ref, home_ref, dw_ref,
    put_ref, get_ref, put_back_ref, get_back_ref, stack_ref,
    xkv, xuq, rkv, ruq, gkv, guq, hkv, huq,
    kv_ref, uq_ref, own_ref, duq_ref, part_ref, back_ref,
    wgt_ref, fac_ref, mask_ref, att_ref, datt_ref, mixed_ref, live_ref, dmix_ref,
    negs_ref, neg_ref, sum_x, sum_r, sum_z, sum_zr, sum_f,
    a2a_send, a2a_recv, neg_send, neg_zrecv, neg_xsend, neg_xrecv,
    halo_send, halo_recv, back_send, back_recv,
    sx_send, sx_recv, sz_send, sz_recv, sf_send, sf_recv,
):
    g = lax.axis_index("dp")
    t = lax.axis_index("seq")
    rows, width = att_ref.shape
    slots = 8 * rows
    head = width // HEADS
    scale = 1.0 / math.sqrt(head)
    per_ring = n_seq // n_dp
    d_rows = width // n_seq
    rb = slots // n_seq
    my_turn = lax.rem(t, n_dp) == g

    def rcopy(src, dst, ssem, rsem, **where):
        return pltpu.make_async_remote_copy(
            src_ref=src, dst_ref=dst, send_sem=ssem, recv_sem=rsem,
            device_id=where, device_id_type=MESH,
        )

    def each_seq_peer(body):
        def step(i, c):
            body(lax.rem(t + i, n_seq))
            return c
        lax.fori_loop(1, n_seq, step, 0)

    def far_first(body):
        half = n_seq // 2

        def step(i, c):
            k = half - i
            body(lax.rem(t + k, n_seq))

            @pl.when(k < half)
            def _():
                body(lax.rem(t + n_seq - k, n_seq))
            return c
        lax.fori_loop(0, half, step, 0)

    def each_dp_peer(body):
        def step(i, c):
            body(lax.rem(g + i, n_dp))
            return c
        lax.fori_loop(1, n_dp, step, 0)

    barrier = pltpu.get_barrier_semaphore()
    each_seq_peer(lambda s: pl.semaphore_signal(barrier, inc=1, device_id={"seq": s}, device_id_type=MESH))
    each_dp_peer(lambda d: pl.semaphore_signal(barrier, inc=1, device_id={"dp": d}, device_id_type=MESH))

    send_f = send_ref[...].astype(F32)
    recv_f = recv_ref[...].astype(F32)
    one = lambda m: jnp.where(m, 1.0, 0.0).astype(BF)

    def build_put(b, c):
        i0 = iota((rows, rows), 0)
        l0 = iota((rows, rows), 1)
        slot = b * (rows // 8) + lax.shift_right_logical(i0, 3)
        idx = jnp.sum(jnp.where(l0 == slot, send_f, 0.0), axis=1, keepdims=True)
        i = iota((rows, slots), 0)
        l = iota((rows, slots), 1)
        m = (idx == (l & (rows - 1)).astype(F32)) & ((i & 7) == lax.shift_right_logical(l, 7))
        put_ref[pl.ds(pl.multiple_of(b * rows, rows), rows), :] = one(m)
        return c

    lax.fori_loop(0, 8, build_put, 0)

    r = iota((16, 512), 0)
    l = iota((16, 512), 1)
    j = r & 3
    pick = jnp.where(j == 0, ids_ref[0], jnp.where(j == 1, ids_ref[1], jnp.where(j == 2, ids_ref[2], ids_ref[3])))
    hit = l == pick
    block = jnp.zeros((16, CH), F32)
    for q in range(4):
        block = block + mm(one(hit & (lax.shift_right_logical(r, 2) == q)), table_ref[:, q * CH:(q + 1) * CH])

    @pl.when(my_turn)
    def _():
        negs_ref[g * per_ring + lax.div(t, n_dp)] = block.astype(BF)

    def stack(ref, starts):
        for n, c in enumerate(starts):
            stack_ref[n * rows:(n + 1) * rows, :] = ref[:, c:c + CH]

    kv_cols = [width + n * CH for n in range(4)] + [3 * width + n * CH for n in range(4)]
    uq_cols = [n * CH for n in range(4)] + [2 * width + n * CH for n in range(4)]
    half_cols = [n * CH for n in range(8)]

    def to_blocks(mat, dst):
        nb = 256 // rb
        for b in range(slots // 256):
            y = mm(mat[b * 256:(b + 1) * 256, :], stack_ref[...]).astype(BF)
            dst[b * nb:(b + 1) * nb] = y.reshape(nb, rb, CH)

    def from_blocks(mat, src, write):
        v = src[...].reshape(slots, CH)
        per = 256 // rows
        for b in range(slots // 256):
            y = mm(mat[b * 256:(b + 1) * 256, :], v).astype(BF)
            for n in range(per):
                write(b * per + n, y[n * rows:(n + 1) * rows])

    def a2a(n, src, dst):
        dst[t] = src[t]
        far_first(lambda s: rcopy(src.at[s], dst.at[t], a2a_send.at[n], a2a_recv.at[n], seq=s).start())

    def take(buf, sem, count):
        v = buf.at[pl.ds(0, count)]
        pltpu.make_async_copy(v, v, sem).wait()

    stack(qkvu_ref, kv_cols)
    to_blocks(put_ref, xkv)

    pl.semaphore_wait(barrier, n_seq - 1 + n_dp - 1)

    @pl.when(my_turn)
    def _():
        mine = negs_ref.at[g * per_ring + lax.div(t, n_dp)]
        far_first(lambda s: rcopy(mine, mine, neg_send, neg_zrecv.at[lax.div(t, n_dp)], seq=s).start())

    a2a(0, xkv, rkv)
    stack(qkvu_ref, uq_cols)
    to_blocks(put_ref, xuq)
    a2a(1, xuq, ruq)

    i0 = iota((rows, rows), 0)
    l0 = iota((rows, rows), 1)
    send_col = jnp.sum(jnp.where(i0 == l0, send_f, 0.0), axis=1, keepdims=True)
    recv_col = jnp.sum(jnp.where(i0 == l0, recv_f, 0.0), axis=1, keepdims=True)

    def build_rows(j, c):
        l = iota((rows, slots), 1)
        i = iota((rows, slots), 0)
        slot = lax.shift_right_logical(l, 3)
        turn = (l & 7) == j
        at = pl.ds(pl.multiple_of(j * rows, rows), rows)
        get_ref[at, :] = one((recv_col == slot.astype(F32)) & turn)
        send_row = jnp.sum(jnp.where(i == slot, send_col, 0.0), axis=0, keepdims=True)
        get_back_ref[at, :] = one((send_row == i.astype(F32)) & turn)
        recv_row = jnp.concatenate([recv_f] * 8, axis=1)
        put_slot = j * (rows // 8) + lax.shift_right_logical(i, 3)
        put_back_ref[at, :] = one((recv_row == put_slot.astype(F32)) & ((i & 7) == lax.shift_right_logical(l, 7)))
        return c

    lax.fori_loop(0, 8, build_rows, 0)

    own_len = len_ref[0, t]
    len_1 = jnp.where(t >= 1, len_ref[0, lax.max(t - 1, 0)], 0)
    len_2 = jnp.where(t >= 2, len_ref[0, lax.max(t - 2, 0)], 0)
    alive = i0 < own_len
    for n, m in enumerate((alive & (l0 <= i0) & (l0 < own_len), alive & (l0 < len_1), alive & (l0 < len_2))):
        mask_ref[:, n * rows:(n + 1) * rows] = jnp.where(m, 1.0 / rows, 0.0)

    live_col = jnp.where(iota(coef_ref.shape, 0) < own_len, 1.0, 0.0)
    live_ref[...] = (coef_ref[...].astype(F32) * live_col).astype(BF)

    for k in range(per_ring):
        @pl.when(k * n_dp + g != t)
        def _():
            v = negs_ref.at[g * per_ring + k]
            pltpu.make_async_copy(v, v, neg_zrecv.at[k]).wait()
    shards = negs_ref.at[pl.ds(g * per_ring, per_ring)]
    each_dp_peer(lambda d: rcopy(shards, shards, neg_xsend, neg_xrecv, dp=d).start())
    take(negs_ref, neg_xrecv, (n_dp - 1) * per_ring)

    n_negs = 4 * n_seq
    flat = negs_ref[...].reshape(16 * n_seq, CH)
    n = iota((n_negs, 16 * n_seq), 0)
    l = iota((n_negs, 16 * n_seq), 1)
    shard = lax.shift_right_logical(n, 2)
    ring_bits = n_dp.bit_length() - 1
    place = ((shard & (n_dp - 1)) * per_ring + lax.shift_right_logical(shard, ring_bits)) * 16 + (n & 3)
    for q in range(4):
        neg_ref[:, q * CH:(q + 1) * CH] = mm(one(l == place + 4 * q), flat).astype(BF)

    head_grad = mm(live_ref[...], neg_ref[...]).astype(BF)
    for b in range(width // CH):
        dmix_ref[:, b * CH:(b + 1) * CH] = mm_nt(head_grad, w_ref[b * CH:(b + 1) * CH, :])

    take(rkv, a2a_recv.at[0], n_seq - 1)

    def write_kv(n, y):
        kv_ref[0, :, n * CH:(n + 1) * CH] = y
    from_blocks(get_ref, rkv, write_kv)
    for lag in range(1, SPAN):
        @pl.when(t + lag < n_seq)
        def _():
            rcopy(kv_ref.at[0], kv_ref.at[lag], halo_send.at[lag - 1], halo_recv.at[lag - 1], seq=lax.rem(t + lag, n_seq)).start()

        @pl.when(t < lag)
        def _():
            kv_ref[lag] = jnp.zeros(kv_ref.shape[1:], BF)

    take(ruq, a2a_recv.at[1], n_seq - 1)

    def write_uq(n, y):
        uq_ref[:, n * CH:(n + 1) * CH] = y
    from_blocks(get_ref, ruq, write_uq)
    for lag in range(1, SPAN):
        @pl.when(t >= lag)
        def _():
            pltpu.make_async_copy(kv_ref.at[lag], kv_ref.at[lag], halo_recv.at[lag - 1]).wait()

    def lanes(h, base=0):
        return pl.ds(pl.multiple_of(base + h * head, head), head)

    def forward(h, c):
        q = uq_ref[:, lanes(h, width)]
        k3 = kv_ref[:, :, lanes(h, width)].reshape(SPAN * rows, head)
        v3 = kv_ref[:, :, lanes(h)].reshape(SPAN * rows, head)
        s = mm_nt(q, k3) * scale
        sig = 0.5 + 0.5 * jnp.tanh(0.5 * s)
        m = mask_ref[...]
        w = (s * sig * m).astype(BF)
        wgt_ref[h] = w
        fac_ref[h] = m * scale * (sig * (1.0 + s * (1.0 - sig)))
        att_ref[:, lanes(h)] = mm(w, v3)
        return c

    lax.fori_loop(0, HEADS, forward, 0)

    step = 32
    for b in range(rows // step):
        at = slice(b * step, (b + 1) * step)
        a = att_ref[at, :]
        cen = a - jnp.mean(a, axis=1, keepdims=True)
        inv = lax.rsqrt(jnp.mean(cen * cen, axis=1, keepdims=True) + eps)
        normed = cen * inv
        u = uq_ref[at, :width].astype(F32)
        mixed_ref[at, :] = (normed * u).astype(BF)
        dm = dmix_ref[at, :]
        duq_ref[at, :width] = (dm * normed).astype(BF)
        dn = dm * u
        da = (dn - jnp.mean(dn, axis=1, keepdims=True) - normed * jnp.mean(dn * normed, axis=1, keepdims=True)) * inv
        datt_ref[at, :] = da.astype(BF)

    def backward(h, c):
        q = uq_ref[:, lanes(h, width)]
        k3 = kv_ref[:, :, lanes(h, width)].reshape(SPAN * rows, head)
        v3 = kv_ref[:, :, lanes(h)].reshape(SPAN * rows, head)
        da = datt_ref[:, lanes(h)]
        ds = (mm_nt(da, v3) * fac_ref[h]).astype(BF)
        duq_ref[:, lanes(h, width)] = mm(ds, k3).astype(BF)
        kp = mm_tn(ds, q)
        vp = mm_tn(wgt_ref[h], da)
        own_ref[:, lanes(h, width)] = kp[:rows]
        own_ref[:, lanes(h)] = vp[:rows]
        for lag in range(1, SPAN):
            part_ref[lag - 1, :, lanes(h, width)] = kp[lag * rows:(lag + 1) * rows].astype(BF)
            part_ref[lag - 1, :, lanes(h)] = vp[lag * rows:(lag + 1) * rows].astype(BF)
        return c

    lax.fori_loop(0, HEADS, backward, 0)

    for lag in range(1, SPAN):
        @pl.when(t >= lag)
        def _():
            rcopy(part_ref.at[lag - 1], back_ref.at[lag - 1], back_send.at[lag - 1], back_recv.at[lag - 1], seq=lax.rem(t + n_seq - lag, n_seq)).start()

        @pl.when(t + lag >= n_seq)
        def _():
            back_ref[lag - 1] = jnp.zeros(back_ref.shape[1:], BF)

    stack(duq_ref, half_cols)
    to_blocks(put_back_ref, guq)
    a2a(2, guq, huq)

    per_block = rows // d_rows
    for b in range(width // rows):
        y = mm_tn(mixed_ref[:, b * rows:(b + 1) * rows], live_ref[...])
        for n in range(per_block):
            s = b * per_block + n
            sum_x[s % n_dp, s // n_dp] = y[n * d_rows:(n + 1) * d_rows]
    sum_r[g] = sum_x[g]
    each_dp_peer(lambda d: rcopy(sum_x.at[d], sum_r.at[g], sx_send, sx_recv, dp=d).start())

    for b in range(width // CH):
        out_ref[:, b * CH:(b + 1) * CH] = mm(mixed_ref[...], w_ref[:, b * CH:(b + 1) * CH]).astype(BF)

    take(sum_r, sx_recv, n_dp - 1)
    sum_z[...] = lax.fori_loop(1, n_dp, lambda i, acc: acc + sum_r[i], sum_r[0])
    for k in range(per_ring):
        s = k * n_dp + g

        @pl.when(s != t)
        def _():
            rcopy(sum_z.at[k], sum_zr.at[t], sz_send.at[k], sz_recv, seq=s).start()

        @pl.when(s == t)
        def _():
            sum_zr[t] = sum_z[k]

    for lag in range(1, SPAN):
        @pl.when(t + lag < n_seq)
        def _():
            pltpu.make_async_copy(back_ref.at[lag - 1], back_ref.at[lag - 1], back_recv.at[lag - 1]).wait()
    for n in range(8):
        c = slice(n * CH, (n + 1) * CH)
        y = own_ref[:, c] + back_ref[0, :, c].astype(F32) + back_ref[1, :, c].astype(F32)
        stack_ref[n * rows:(n + 1) * rows, :] = y.astype(BF)
    to_blocks(put_back_ref, gkv)
    a2a(3, gkv, hkv)

    @pl.when(my_turn)
    def _():
        take(sum_zr, sz_recv, n_seq - 1)
        sum_f[...] = lax.fori_loop(1, n_seq, lambda i, acc: acc + sum_zr[i], sum_zr[0])
        each_dp_peer(lambda d: rcopy(sum_f, sum_f, sf_send, sf_recv, dp=d).start())

    @pl.when(jnp.logical_not(my_turn))
    def _():
        pltpu.make_async_copy(sum_f, sum_f, sf_recv).wait()

    total = sum_f[...]
    top = total.astype(BF)
    low = (total - top.astype(F32)).astype(BF)
    cols = width // n_dp
    if cols >= 128:
        nb = neg_ref[:, pl.ds(pl.multiple_of(g * cols, cols), cols)]
        dw_ref[...] = mm(top, nb) + mm(low, nb)
    else:
        per = 128 // cols
        nb = neg_ref[:, pl.ds(pl.multiple_of(lax.div(g, per) * 128, 128), 128)]
        y = mm(top, nb) + mm(low, nb)
        z = y[:, :cols]
        for n in range(1, per):
            z = jnp.where(lax.rem(g, per) == n, y[:, n * cols:(n + 1) * cols], z)
        dw_ref[...] = z

    take(huq, a2a_recv.at[2], n_seq - 1)

    def home_uq(n, y):
        home_ref[:, uq_cols[n]:uq_cols[n] + CH] = y
    from_blocks(get_back_ref, huq, home_uq)
    take(hkv, a2a_recv.at[3], n_seq - 1)

    def home_kv(n, y):
        home_ref[:, kv_cols[n]:kv_cols[n] + CH] = y
    from_blocks(get_back_ref, hkv, home_kv)

    for n, buf in enumerate((xkv, xuq, guq, gkv)):
        take(buf, a2a_send.at[n], n_seq - 1)

    def sent(buf, sem):
        pltpu.make_async_copy(buf, buf, sem).wait()

    take(negs_ref, neg_xsend, (n_dp - 1) * per_ring)
    take(sum_x, sx_send, n_dp - 1)

    @pl.when(my_turn)
    def _():
        take(negs_ref, neg_send, n_seq - 1)
        take(sum_zr, sf_send, n_dp - 1)

    for k in range(per_ring):
        @pl.when(k * n_dp + g != t)
        def _():
            sent(sum_z.at[k], sz_send.at[k])
    for lag in range(1, SPAN):
        @pl.when(t + lag < n_seq)
        def _():
            sent(kv_ref.at[0], halo_send.at[lag - 1])

        @pl.when(t >= lag)
        def _():
            sent(part_ref.at[lag - 1], back_send.at[lag - 1])


def on_device(n_dp, n_seq, qkvu, w_out, head_coef, item_table, neg_ids, send_order, recv_order, tile_len):
    rows = qkvu.shape[0]
    width = w_out.shape[0]
    slots = 8 * rows
    rb = slots // n_seq
    per_ring = n_seq // n_dp
    d_rows = width // n_seq
    negs = head_coef.shape[1]
    vm = pl.BlockSpec(memory_space=pltpu.VMEM)
    sm = pl.BlockSpec(memory_space=pltpu.SMEM)
    dma = pltpu.SemaphoreType.DMA
    blocks = pltpu.VMEM((n_seq, rb, CH), BF)
    square = pltpu.VMEM((slots, slots), BF)
    return pl.pallas_call(
        functools.partial(kernel, n_dp, n_seq),
        out_shape=(
            jax.ShapeDtypeStruct((rows, width), BF),
            jax.ShapeDtypeStruct((rows, 4 * width), BF),
            jax.ShapeDtypeStruct((d_rows, width // n_dp), F32),
        ),
        in_specs=[sm, sm] + [vm] * 6,
        out_specs=(vm, vm, vm),
        scratch_shapes=[
            square, square, square, square, pltpu.VMEM((slots, CH), BF),
            blocks, blocks, blocks, blocks, blocks, blocks, blocks, blocks,
            pltpu.VMEM((SPAN, rows, 2 * width), BF),
            pltpu.VMEM((rows, 2 * width), BF),
            pltpu.VMEM((rows, 2 * width), F32),
            pltpu.VMEM((rows, 2 * width), BF),
            pltpu.VMEM((SPAN - 1, rows, 2 * width), BF),
            pltpu.VMEM((SPAN - 1, rows, 2 * width), BF),
            pltpu.VMEM((HEADS, rows, SPAN * rows), BF),
            pltpu.VMEM((HEADS, rows, SPAN * rows), F32),
            pltpu.VMEM((rows, SPAN * rows), F32),
            pltpu.VMEM((rows, width), F32),
            pltpu.VMEM((rows, width), BF),
            pltpu.VMEM((rows, width), BF),
            pltpu.VMEM((rows, negs), BF),
            pltpu.VMEM((rows, width), F32),
            pltpu.VMEM((n_seq, 16, CH), BF),
            pltpu.VMEM((negs, width), BF),
            pltpu.VMEM((n_dp, per_ring, d_rows, negs), F32),
            pltpu.VMEM((n_dp, per_ring, d_rows, negs), F32),
            pltpu.VMEM((per_ring, d_rows, negs), F32),
            pltpu.VMEM((n_seq, d_rows, negs), F32),
            pltpu.VMEM((d_rows, negs), F32),
            dma((4,)), dma((4,)), dma, dma((per_ring,)), dma, dma,
            dma((SPAN - 1,)), dma((SPAN - 1,)), dma((SPAN - 1,)), dma((SPAN - 1,)),
            dma, dma, dma((per_ring,)), dma, dma, dma,
        ],
        compiler_params=pltpu.CompilerParams(
            collective_id=0, has_side_effects=True, vmem_limit_bytes=60 * 2**20
        ),
    )(neg_ids, tile_len, qkvu, w_out, head_coef, item_table, send_order, recv_order)


def solution(mesh):
    placed = (
        P(("dp", "seq"), None),
        P(),
        P(("dp", "seq"), None),
        P("seq", None),
        P("seq"),
        P(("dp", "seq"), None),
        P(("dp", "seq"), None),
        P("dp", None),
    )
    return jax.shard_map(
        functools.partial(on_device, mesh.shape["dp"], mesh.shape["seq"]),
        mesh=mesh,
        in_specs=placed,
        out_specs=(P(("dp", "seq"), None), P(("dp", "seq"), None), P("seq", "dp")),
        check_vma=False,
    )
```

```python
import functools
import math

import jax
import jax.numpy as jnp
from jax import lax
from jax.experimental import pallas as pl
from jax.experimental.pallas import tpu as pltpu
from jax.sharding import PartitionSpec as P

HEADS = 8
SPAN = 3
CH = 256
eps = 1e-05
BF = jnp.bfloat16
F32 = jnp.float32
MESH = pl.DeviceIdType.MESH


def iota(shape, dim):
    return lax.broadcasted_iota(jnp.int32, shape, dim)


def mm(a, b):
    return jnp.dot(a, b, preferred_element_type=F32)


def mm_nt(a, b):
    return lax.dot_general(a, b, (((1,), (1,)), ((), ())), preferred_element_type=F32)


def mm_tn(a, b):
    return lax.dot_general(a, b, (((0,), (0,)), ((), ())), preferred_element_type=F32)


def kernel(
    n_dp, n_seq,
    ids_ref, len_ref, qkvu_ref, coef_ref, send_ref, recv_ref, w_hbm, table_hbm,
    out_ref, home_ref, dw_ref,
    w_ref, table_ref,
    put_ref, get_ref, put_back_ref, get_back_ref, stack_ref, pair_ref, thin_ref,
    xkv, rkv, gkv, hkv,
    xq, xu, rq, ru, gq, gu, hq, hu,
    kv_ref, q_ref, u_ref, own_ref, part_ref, back_ref,
    wgt_ref, fac_ref, mask_ref, att_ref, inv_ref, datt_ref, mixed_ref, live_ref, dmix_ref,
    negs_ref, neg_ref, sum_x, sum_r, sum_z, sum_zr, sum_f,
    load_sem, a2a_send, a2a_recv, neg_send, neg_zrecv, neg_xsend, neg_xrecv,
    halo_send, halo_recv, back_send, back_recv,
    sx_send, sx_recv, sz_send, sz_recv, sf_send, sf_recv,
):
    g = lax.axis_index("dp")
    t = lax.axis_index("seq")
    rows, width = att_ref.shape
    slots = 8 * rows
    head = width // HEADS
    scale = 1.0 / math.sqrt(head)
    per_ring = n_seq // n_dp
    d_rows = width // n_seq
    rb = slots // n_seq
    my_turn = lax.rem(t, n_dp) == g

    def rcopy(src, dst, ssem, rsem, **where):
        return pltpu.make_async_remote_copy(
            src_ref=src, dst_ref=dst, send_sem=ssem, recv_sem=rsem,
            device_id=where, device_id_type=MESH,
        )

    def each_seq_peer(body):
        def step(i, c):
            body(lax.rem(t + i, n_seq))
            return c
        lax.fori_loop(1, n_seq, step, 0)

    def far_first(body):
        half = n_seq // 2

        def step(i, c):
            k = half - i
            body(lax.rem(t + k, n_seq))

            @pl.when(k < half)
            def _():
                body(lax.rem(t + n_seq - k, n_seq))
            return c
        lax.fori_loop(0, half, step, 0)

    def each_dp_peer(body):
        def step(i, c):
            body(lax.rem(g + i, n_dp))
            return c
        lax.fori_loop(1, n_dp, step, 0)

    barrier = pltpu.get_barrier_semaphore()
    each_seq_peer(lambda s: pl.semaphore_signal(barrier, inc=1, device_id={"seq": s}, device_id_type=MESH))
    each_dp_peer(lambda d: pl.semaphore_signal(barrier, inc=1, device_id={"dp": d}, device_id_type=MESH))

    load_table = pltpu.make_async_copy(table_hbm, table_ref, load_sem.at[0])
    load_w = pltpu.make_async_copy(w_hbm, w_ref, load_sem.at[1])
    load_table.start()
    load_w.start()

    send_f = send_ref[...].astype(F32)
    recv_f = recv_ref[...].astype(F32)
    one = lambda m: jnp.where(m, 1.0, 0.0).astype(BF)

    def build_put(b, c):
        i0 = iota((rows, rows), 0)
        l0 = iota((rows, rows), 1)
        slot = b * (rows // 8) + lax.shift_right_logical(i0, 3)
        idx = jnp.sum(jnp.where(l0 == slot, send_f, 0.0), axis=1, keepdims=True)
        i = iota((rows, slots), 0)
        l = iota((rows, slots), 1)
        m = (idx == (l & (rows - 1)).astype(F32)) & ((i & 7) == lax.shift_right_logical(l, 7))
        put_ref[pl.ds(pl.multiple_of(b * rows, rows), rows), :] = one(m)
        return c

    lax.fori_loop(0, 8, build_put, 0)

    def stack(starts):
        for n, c in enumerate(starts):
            stack_ref[n * rows:(n + 1) * rows, :] = qkvu_ref[:, c:c + CH]

    kv_cols = [width + n * CH for n in range(4)] + [3 * width + n * CH for n in range(4)]

    def to_blocks(mat, src, *dsts):
        nb = 256 // rb
        for b in range(slots // 256):
            y = mm(mat[b * 256:(b + 1) * 256, :], src[...]).astype(BF)
            w = y.shape[1] // len(dsts)
            for n, dst in enumerate(dsts):
                dst[b * nb:(b + 1) * nb] = y[:, n * w:(n + 1) * w].reshape(nb, rb, w)

    def from_blocks(mat, v, write):
        v = v.reshape(slots, v.shape[-1])
        per = 256 // rows
        for b in range(slots // 256):
            y = mm(mat[b * 256:(b + 1) * 256, :], v).astype(BF)
            for n in range(per):
                write(b * per + n, y[n * rows:(n + 1) * rows])

    def a2a(n, src, dst):
        dst[t] = src[t]
        far_first(lambda s: rcopy(src.at[s], dst.at[t], a2a_send.at[n], a2a_recv.at[n], seq=s).start())

    def take(buf, sem, count):
        v = buf.at[pl.ds(0, count)]
        pltpu.make_async_copy(v, v, sem).wait()

    def whole(buf, sem):
        pltpu.make_async_copy(buf, buf, sem).wait()

    stack(kv_cols)
    to_blocks(put_ref, stack_ref, xkv)

    pl.semaphore_wait(barrier, n_seq - 1 + n_dp - 1)
    a2a(0, xkv, rkv)

    load_table.wait()
    r = iota((16, 512), 0)
    l = iota((16, 512), 1)
    j = r & 3
    pick = jnp.where(j == 0, ids_ref[0], jnp.where(j == 1, ids_ref[1], jnp.where(j == 2, ids_ref[2], ids_ref[3])))
    hit = l == pick
    block = jnp.zeros((16, CH), F32)
    for q in range(4):
        block = block + mm(one(hit & (lax.shift_right_logical(r, 2) == q)), table_ref[:, q * CH:(q + 1) * CH])

    @pl.when(my_turn)
    def _():
        negs_ref[g * per_ring + lax.div(t, n_dp)] = block.astype(BF)
        mine = negs_ref.at[g * per_ring + lax.div(t, n_dp)]
        far_first(lambda s: rcopy(mine, mine, neg_send, neg_zrecv.at[lax.div(t, n_dp)], seq=s).start())

    for n in range(8):
        pair_ref[n * rows:(n + 1) * rows, :head] = qkvu_ref[:, 2 * width + n * head:2 * width + (n + 1) * head]
        pair_ref[n * rows:(n + 1) * rows, head:] = qkvu_ref[:, n * head:(n + 1) * head]
    to_blocks(put_ref, pair_ref, xq, xu)
    a2a(1, xq, rq)

    i0 = iota((rows, rows), 0)
    l0 = iota((rows, rows), 1)
    send_col = jnp.sum(jnp.where(i0 == l0, send_f, 0.0), axis=1, keepdims=True)
    recv_col = jnp.sum(jnp.where(i0 == l0, recv_f, 0.0), axis=1, keepdims=True)

    def build_rows(j, c):
        l = iota((rows, slots), 1)
        i = iota((rows, slots), 0)
        slot = lax.shift_right_logical(l, 3)
        turn = (l & 7) == j
        at = pl.ds(pl.multiple_of(j * rows, rows), rows)
        get_ref[at, :] = one((recv_col == slot.astype(F32)) & turn)
        send_row = jnp.sum(jnp.where(i == slot, send_col, 0.0), axis=0, keepdims=True)
        get_back_ref[at, :] = one((send_row == i.astype(F32)) & turn)
        recv_row = jnp.concatenate([recv_f] * 8, axis=1)
        put_slot = j * (rows // 8) + lax.shift_right_logical(i, 3)
        put_back_ref[at, :] = one((recv_row == put_slot.astype(F32)) & ((i & 7) == lax.shift_right_logical(l, 7)))
        return c

    lax.fori_loop(0, 8, build_rows, 0)

    own_len = len_ref[0, t]
    len_1 = jnp.where(t >= 1, len_ref[0, lax.max(t - 1, 0)], 0)
    len_2 = jnp.where(t >= 2, len_ref[0, lax.max(t - 2, 0)], 0)
    alive = i0 < own_len
    for n, m in enumerate((alive & (l0 <= i0) & (l0 < own_len), alive & (l0 < len_1), alive & (l0 < len_2))):
        mask_ref[:, n * rows:(n + 1) * rows] = jnp.where(m, 1.0 / rows, 0.0)

    live_col = jnp.where(iota(coef_ref.shape, 0) < own_len, 1.0, 0.0)
    live_ref[...] = (coef_ref[...].astype(F32) * live_col).astype(BF)

    take(rkv, a2a_recv.at[0], n_seq - 1)

    def write_kv(n, y):
        kv_ref[0, :, n * CH:(n + 1) * CH] = y
    from_blocks(get_ref, rkv[...], write_kv)
    odd = lax.rem(t, 2) == 1
    even = lax.rem(t, 2) == 0
    mate = t + 1 - 2 * lax.rem(t, 2)

    @pl.when(t + 2 < n_seq)
    def _():
        rcopy(kv_ref.at[0], kv_ref.at[2], halo_send.at[1], halo_recv.at[1], seq=lax.rem(t + 2, n_seq)).start()

    @pl.when(even)
    def _():
        rcopy(kv_ref.at[0], kv_ref.at[1], halo_send.at[0], halo_recv.at[0], seq=mate).start()

    for lag in range(1, SPAN):
        @pl.when(t < lag)
        def _():
            kv_ref[lag] = jnp.zeros(kv_ref.shape[1:], BF)

    a2a(2, xu, ru)

    for k in range(per_ring):
        @pl.when(k * n_dp + g != t)
        def _():
            whole(negs_ref.at[g * per_ring + k], neg_zrecv.at[k])
    shards = negs_ref.at[pl.ds(g * per_ring, per_ring)]
    each_dp_peer(lambda d: rcopy(shards, shards, neg_xsend, neg_xrecv, dp=d).start())
    take(negs_ref, neg_xrecv, (n_dp - 1) * per_ring)

    n_negs = 4 * n_seq
    flat = negs_ref[...].reshape(16 * n_seq, CH)
    n = iota((n_negs, 16 * n_seq), 0)
    l = iota((n_negs, 16 * n_seq), 1)
    shard = lax.shift_right_logical(n, 2)
    ring_bits = n_dp.bit_length() - 1
    place = ((shard & (n_dp - 1)) * per_ring + lax.shift_right_logical(shard, ring_bits)) * 16 + (n & 3)
    for q in range(4):
        neg_ref[:, q * CH:(q + 1) * CH] = mm(one(l == place + 4 * q), flat).astype(BF)

    load_w.wait()
    head_grad = mm(live_ref[...], neg_ref[...]).astype(BF)
    for b in range(width // CH):
        dmix_ref[:, b * CH:(b + 1) * CH] = mm_nt(head_grad, w_ref[b * CH:(b + 1) * CH, :])

    take(rq, a2a_recv.at[1], n_seq - 1)

    def write_q(n, y):
        q_ref[:, n * head:(n + 1) * head] = y
    from_blocks(get_ref, rq[...], write_q)

    @pl.when(t >= 2)
    def _():
        whole(kv_ref.at[2], halo_recv.at[1])

    @pl.when(odd & (t >= 2))
    def _():
        rcopy(kv_ref.at[2], kv_ref.at[1], halo_send.at[0], halo_recv.at[0], seq=mate).start()

    @pl.when(t >= 1)
    def _():
        whole(kv_ref.at[1], halo_recv.at[0])

    def lanes(h, base=0):
        return pl.ds(pl.multiple_of(base + h * head, head), head)

    def forward(h, c):
        q = q_ref[:, lanes(h)]
        k3 = kv_ref[:, :, lanes(h, width)].reshape(SPAN * rows, head)
        v3 = kv_ref[:, :, lanes(h)].reshape(SPAN * rows, head)
        s = mm_nt(q, k3) * scale
        sig = 0.5 + 0.5 * jnp.tanh(0.5 * s)
        m = mask_ref[...]
        w = (s * sig * m).astype(BF)
        wgt_ref[h] = w
        fac_ref[h] = m * scale * (sig * (1.0 + s * (1.0 - sig)))
        att_ref[:, lanes(h)] = mm(w, v3)
        return c

    lax.fori_loop(0, HEADS, forward, 0)

    step = 32
    spans = [slice(b * step, (b + 1) * step) for b in range(rows // step)]
    for at in spans:
        a = att_ref[at, :]
        cen = a - jnp.mean(a, axis=1, keepdims=True)
        inv = lax.rsqrt(jnp.mean(cen * cen, axis=1, keepdims=True) + eps)
        normed = cen * inv
        att_ref[at, :] = normed
        inv_ref[at, :] = jnp.broadcast_to(inv, (step, 128))
        du = (dmix_ref[at, :] * normed).astype(BF)
        for n in range(8):
            thin_ref[n * rows + at.start:n * rows + at.stop, :] = du[:, n * head:(n + 1) * head]
    to_blocks(put_back_ref, thin_ref, gu)
    a2a(3, gu, hu)

    take(ru, a2a_recv.at[2], n_seq - 1)

    def write_u(n, y):
        u_ref[:, n * head:(n + 1) * head] = y
    from_blocks(get_ref, ru[...], write_u)

    for at in spans:
        normed = att_ref[at, :]
        inv = inv_ref[at, :1]
        u = u_ref[at, :].astype(F32)
        mixed_ref[at, :] = (normed * u).astype(BF)
        dn = dmix_ref[at, :] * u
        da = (dn - jnp.mean(dn, axis=1, keepdims=True) - normed * jnp.mean(dn * normed, axis=1, keepdims=True)) * inv
        datt_ref[at, :] = da.astype(BF)

    def backward(h, c):
        q = q_ref[:, lanes(h)]
        k3 = kv_ref[:, :, lanes(h, width)].reshape(SPAN * rows, head)
        v3 = kv_ref[:, :, lanes(h)].reshape(SPAN * rows, head)
        da = datt_ref[:, lanes(h)]
        ds = (mm_nt(da, v3) * fac_ref[h]).astype(BF)
        thin_ref[pl.ds(pl.multiple_of(h * rows, rows), rows), :] = mm(ds, k3).astype(BF)
        kp = mm_tn(ds, q)
        vp = mm_tn(wgt_ref[h], da)
        own_ref[:, lanes(h, width)] = kp[:rows]
        own_ref[:, lanes(h)] = vp[:rows]
        for lag in range(1, SPAN):
            part_ref[lag - 1, :, lanes(h, width)] = kp[lag * rows:(lag + 1) * rows].astype(BF)
            part_ref[lag - 1, :, lanes(h)] = vp[lag * rows:(lag + 1) * rows].astype(BF)
        return c

    lax.fori_loop(0, HEADS, backward, 0)

    swap = rcopy(part_ref.at[0], back_ref.at[0], back_send.at[0], back_recv.at[0], seq=mate)
    swap.start()

    def hand_back():
        rcopy(part_ref.at[1], back_ref.at[1], back_send.at[1], back_recv.at[1], seq=lax.rem(t + n_seq - 2, n_seq)).start()

    @pl.when(even & (t >= 2))
    def _():
        hand_back()

    @pl.when(t + 2 >= n_seq)
    def _():
        back_ref[1] = jnp.zeros(back_ref.shape[1:], BF)

    per_block = rows // d_rows
    for b in range(width // rows):
        y = mm_tn(mixed_ref[:, b * rows:(b + 1) * rows], live_ref[...])
        for n in range(per_block):
            s = b * per_block + n
            sum_x[s % n_dp, s // n_dp] = y[n * d_rows:(n + 1) * d_rows]
    sum_r[g] = sum_x[g]
    each_dp_peer(lambda d: rcopy(sum_x.at[d], sum_r.at[g], sx_send, sx_recv, dp=d).start())

    whole(back_ref.at[0], back_recv.at[0])

    @pl.when(odd & (t >= 2))
    def _():
        part_ref[1] = (part_ref[1].astype(F32) + back_ref[0].astype(F32)).astype(BF)
        hand_back()

    to_blocks(put_back_ref, thin_ref, gq)
    a2a(4, gq, hq)

    take(sum_r, sx_recv, n_dp - 1)
    sum_z[...] = lax.fori_loop(1, n_dp, lambda i, acc: acc + sum_r[i], sum_r[0])
    for k in range(per_ring):
        s = k * n_dp + g

        @pl.when(s != t)
        def _():
            rcopy(sum_z.at[k], sum_zr.at[t], sz_send.at[k], sz_recv, seq=s).start()

        @pl.when(s == t)
        def _():
            sum_zr[t] = sum_z[k]

    @pl.when(t + 2 < n_seq)
    def _():
        whole(back_ref.at[1], back_recv.at[1])
    keep = jnp.where(even, 1.0, 0.0)
    for n in range(8):
        c = slice(n * CH, (n + 1) * CH)
        y = own_ref[:, c] + back_ref[0, :, c].astype(F32) * keep + back_ref[1, :, c].astype(F32)
        stack_ref[n * rows:(n + 1) * rows, :] = y.astype(BF)
    to_blocks(put_back_ref, stack_ref, gkv)
    a2a(5, gkv, hkv)

    for b in range(width // CH):
        out_ref[:, b * CH:(b + 1) * CH] = mm(mixed_ref[...], w_ref[:, b * CH:(b + 1) * CH]).astype(BF)

    @pl.when(my_turn)
    def _():
        take(sum_zr, sz_recv, n_seq - 1)
        sum_f[...] = lax.fori_loop(1, n_seq, lambda i, acc: acc + sum_zr[i], sum_zr[0])
        each_dp_peer(lambda d: rcopy(sum_f, sum_f, sf_send, sf_recv, dp=d).start())

    @pl.when(jnp.logical_not(my_turn))
    def _():
        whole(sum_f, sf_recv)

    total = sum_f[...]
    top = total.astype(BF)
    low = (total - top.astype(F32)).astype(BF)
    cols = width // n_dp
    if cols >= 128:
        nb = neg_ref[:, pl.ds(pl.multiple_of(g * cols, cols), cols)]
        dw_ref[...] = mm(top, nb) + mm(low, nb)
    else:
        per = 128 // cols
        nb = neg_ref[:, pl.ds(pl.multiple_of(lax.div(g, per) * 128, 128), 128)]
        y = mm(top, nb) + mm(low, nb)
        z = y[:, :cols]
        for n in range(1, per):
            z = jnp.where(lax.rem(g, per) == n, y[:, n * cols:(n + 1) * cols], z)
        dw_ref[...] = z

    take(hu, a2a_recv.at[3], n_seq - 1)
    take(hq, a2a_recv.at[4], n_seq - 1)

    def home_uq(n, y):
        home_ref[:, n * head:(n + 1) * head] = y[:, :head]
        home_ref[:, 2 * width + n * head:2 * width + (n + 1) * head] = y[:, head:]
    both = jnp.concatenate([hu[...].reshape(slots, head), hq[...].reshape(slots, head)], axis=1)
    from_blocks(get_back_ref, both, home_uq)

    for n, buf in enumerate((xkv, xq, xu, gu, gq)):
        take(buf, a2a_send.at[n], n_seq - 1)
    take(negs_ref, neg_xsend, (n_dp - 1) * per_ring)
    take(sum_x, sx_send, n_dp - 1)

    @pl.when(my_turn)
    def _():
        take(negs_ref, neg_send, n_seq - 1)
        take(sum_zr, sf_send, n_dp - 1)

    for k in range(per_ring):
        @pl.when(k * n_dp + g != t)
        def _():
            whole(sum_z.at[k], sz_send.at[k])

    @pl.when(t + 2 < n_seq)
    def _():
        whole(kv_ref.at[0], halo_send.at[1])

    @pl.when(even | (t >= 2))
    def _():
        whole(kv_ref.at[0], halo_send.at[0])
    whole(part_ref.at[0], back_send.at[0])

    @pl.when(t >= 2)
    def _():
        whole(part_ref.at[1], back_send.at[1])

    take(hkv, a2a_recv.at[5], n_seq - 1)

    def home_kv(n, y):
        home_ref[:, kv_cols[n]:kv_cols[n] + CH] = y
    from_blocks(get_back_ref, hkv[...], home_kv)
    take(gkv, a2a_send.at[5], n_seq - 1)


def on_device(n_dp, n_seq, qkvu, w_out, head_coef, item_table, neg_ids, send_order, recv_order, tile_len):
    rows = qkvu.shape[0]
    width = w_out.shape[0]
    slots = 8 * rows
    rb = slots // n_seq
    per_ring = n_seq // n_dp
    d_rows = width // n_seq
    negs = head_coef.shape[1]
    vm = pl.BlockSpec(memory_space=pltpu.VMEM)
    sm = pl.BlockSpec(memory_space=pltpu.SMEM)
    dma = pltpu.SemaphoreType.DMA
    any_space = pl.BlockSpec(memory_space=pl.ANY)
    wide = pltpu.VMEM((n_seq, rb, CH), BF)
    thin = pltpu.VMEM((n_seq, rb, CH // 2), BF)
    square = pltpu.VMEM((slots, slots), BF)
    return pl.pallas_call(
        functools.partial(kernel, n_dp, n_seq),
        out_shape=(
            pltpu.VMEM((rows, width), BF),
            pltpu.VMEM((rows, 4 * width), BF),
            pltpu.VMEM((d_rows, width // n_dp), F32),
        ),
        in_specs=[sm, sm, vm, vm, vm, vm, any_space, any_space],
        out_specs=(vm, vm, vm),
        scratch_shapes=[
            pltpu.VMEM(w_out.shape, BF), pltpu.VMEM(item_table.shape, BF),
            square, square, square, square,
            pltpu.VMEM((slots, CH), BF), pltpu.VMEM((slots, CH), BF), pltpu.VMEM((slots, CH // 2), BF),
            wide, wide, wide, wide,
            thin, thin, thin, thin, thin, thin, thin, thin,
            pltpu.VMEM((SPAN, rows, 2 * width), BF),
            pltpu.VMEM((rows, width), BF),
            pltpu.VMEM((rows, width), BF),
            pltpu.VMEM((rows, 2 * width), F32),
            pltpu.VMEM((SPAN - 1, rows, 2 * width), BF),
            pltpu.VMEM((SPAN - 1, rows, 2 * width), BF),
            pltpu.VMEM((HEADS, rows, SPAN * rows), BF),
            pltpu.VMEM((HEADS, rows, SPAN * rows), F32),
            pltpu.VMEM((rows, SPAN * rows), F32),
            pltpu.VMEM((rows, width), F32),
            pltpu.VMEM((rows, 128), F32),
            pltpu.VMEM((rows, width), BF),
            pltpu.VMEM((rows, width), BF),
            pltpu.VMEM((rows, negs), BF),
            pltpu.VMEM((rows, width), F32),
            pltpu.VMEM((n_seq, 16, CH), BF),
            pltpu.VMEM((negs, width), BF),
            pltpu.VMEM((n_dp, per_ring, d_rows, negs), F32),
            pltpu.VMEM((n_dp, per_ring, d_rows, negs), F32),
            pltpu.VMEM((per_ring, d_rows, negs), F32),
            pltpu.VMEM((n_seq, d_rows, negs), F32),
            pltpu.VMEM((d_rows, negs), F32),
            dma((2,)), dma((6,)), dma((6,)), dma, dma((per_ring,)), dma, dma,
            dma((SPAN - 1,)), dma((SPAN - 1,)), dma((SPAN - 1,)), dma((SPAN - 1,)),
            dma, dma, dma((per_ring,)), dma, dma, dma,
        ],
        compiler_params=pltpu.CompilerParams(
            collective_id=0, has_side_effects=True, vmem_limit_bytes=60 * 2**20
        ),
    )(neg_ids, tile_len, qkvu, head_coef, send_order, recv_order, w_out, item_table)


def solution(mesh):
    placed = (
        P(("dp", "seq"), None),
        P(),
        P(("dp", "seq"), None),
        P("seq", None),
        P("seq"),
        P(("dp", "seq"), None),
        P(("dp", "seq"), None),
        P("dp", None),
    )
    return jax.shard_map(
        functools.partial(on_device, mesh.shape["dp"], mesh.shape["seq"]),
        mesh=mesh,
        in_specs=placed,
        out_specs=(P(("dp", "seq"), None), P(("dp", "seq"), None), P("seq", "dp")),
        check_vma=False,
    )
```

```python
import functools
import math

import jax
import jax.numpy as jnp
from jax import lax
from jax.experimental import pallas as pl
from jax.experimental.pallas import tpu as pltpu
from jax.sharding import PartitionSpec as P

HEADS = 8
SPAN = 3
CH = 256
eps = 1e-05
BF = jnp.bfloat16
F32 = jnp.float32
MESH = pl.DeviceIdType.MESH


def iota(shape, dim):
    return lax.broadcasted_iota(jnp.int32, shape, dim)


def mm(a, b):
    return jnp.dot(a, b, preferred_element_type=F32)


def mm_nt(a, b):
    return lax.dot_general(a, b, (((1,), (1,)), ((), ())), preferred_element_type=F32)


def mm_tn(a, b):
    return lax.dot_general(a, b, (((0,), (0,)), ((), ())), preferred_element_type=F32)


def kernel(
    n_dp, n_seq,
    ids_ref, len_ref, qkvu_hbm, coef_hbm, send_hbm, recv_hbm, w_hbm, table_hbm,
    out_ref, home_ref, dw_ref,
    send_ref, recv_ref, qkvu_ref, coef_ref, table_ref, w_ref,
    put_ref, get_ref, put_back_ref, get_back_ref, stack_ref, pair_ref, thin_ref,
    xkv, rkv, gkv, hkv,
    xq, xu, rq, ru, gq, gu, hq, hu,
    kv_ref, q_ref, u_ref, own_ref, part_ref, back_ref,
    wgt_ref, fac_ref, mask_ref, att_ref, inv_ref, datt_ref, mixed_ref, live_ref, dmix_ref,
    negs_ref, neg_ref, sum_x, sum_r, sum_z, sum_zr, sum_f,
    load_sem, a2a_send, a2a_recv, neg_send, neg_zrecv, neg_xsend, neg_xrecv,
    halo_send, halo_recv, back_send, back_recv,
    sx_send, sx_recv, sz_send, sz_recv, sf_send, sf_recv,
):
    g = lax.axis_index("dp")
    t = lax.axis_index("seq")
    rows, width = att_ref.shape
    slots = 8 * rows
    head = width // HEADS
    scale = 1.0 / math.sqrt(head)
    plane = 2 * n_dp
    per_ring = n_seq // plane
    d_rows = width // n_seq
    rb = slots // n_seq
    carrier = 2 * g + lax.rem(t, 2)
    mate = t + 1 - 2 * lax.rem(t, 2)
    my_turn = lax.rem(lax.div(t, 2), n_dp) == g

    def rcopy(src, dst, ssem, rsem, **where):
        return pltpu.make_async_remote_copy(
            src_ref=src, dst_ref=dst, send_sem=ssem, recv_sem=rsem,
            device_id=where, device_id_type=MESH,
        )

    def each_seq_peer(body):
        def step(i, c):
            body(lax.rem(t + i, n_seq))
            return c
        lax.fori_loop(1, n_seq, step, 0)

    def far_first(body):
        half = n_seq // 2

        def step(i, c):
            k = half - i
            body(lax.rem(t + k, n_seq))

            @pl.when(k < half)
            def _():
                body(lax.rem(t + n_seq - k, n_seq))
            return c
        lax.fori_loop(0, half, step, 0)

    def each_dp_peer(body):
        def step(i, c):
            body(lax.rem(g + i, n_dp))
            return c
        lax.fori_loop(1, n_dp, step, 0)

    def each_plane_peer(copy):
        def step(i, c):
            d = lax.rem(g + i, n_dp)

            @pl.when(i > 0)
            def _():
                copy(2 * d + lax.rem(t, 2), {"dp": d}).start()
            copy(2 * d + 1 - lax.rem(t, 2), {"dp": d, "seq": mate}).start()
            return c
        lax.fori_loop(0, n_dp, step, 0)

    loads = [
        pltpu.make_async_copy(src, dst, load_sem.at[n])
        for n, (src, dst) in enumerate((
            (send_hbm, send_ref), (recv_hbm, recv_ref), (qkvu_hbm, qkvu_ref),
            (coef_hbm, coef_ref), (table_hbm, table_ref), (w_hbm, w_ref),
        ))
    ]
    for load in loads:
        load.start()

    barrier = pltpu.get_barrier_semaphore()
    each_seq_peer(lambda s: pl.semaphore_signal(barrier, inc=1, device_id={"seq": s}, device_id_type=MESH))
    each_dp_peer(lambda d: pl.semaphore_signal(barrier, inc=1, device_id={"dp": d}, device_id_type=MESH))
    each_dp_peer(lambda d: pl.semaphore_signal(barrier, inc=1, device_id={"dp": d, "seq": mate}, device_id_type=MESH))

    loads[0].wait()
    loads[1].wait()

    send_f = send_ref[...].astype(F32)
    recv_f = recv_ref[...].astype(F32)
    one = lambda m: jnp.where(m, 1.0, 0.0).astype(BF)

    def build_put(b, c):
        i0 = iota((rows, rows), 0)
        l0 = iota((rows, rows), 1)
        slot = b * (rows // 8) + lax.shift_right_logical(i0, 3)
        idx = jnp.sum(jnp.where(l0 == slot, send_f, 0.0), axis=1, keepdims=True)
        i = iota((rows, slots), 0)
        l = iota((rows, slots), 1)
        m = (idx == (l & (rows - 1)).astype(F32)) & ((i & 7) == lax.shift_right_logical(l, 7))
        put_ref[pl.ds(pl.multiple_of(b * rows, rows), rows), :] = one(m)
        return c

    lax.fori_loop(0, 8, build_put, 0)

    def stack(starts):
        for n, c in enumerate(starts):
            stack_ref[n * rows:(n + 1) * rows, :] = qkvu_ref[:, c:c + CH]

    kv_cols = [width + n * CH for n in range(4)] + [3 * width + n * CH for n in range(4)]

    def to_blocks(mat, src, *dsts):
        nb = 256 // rb
        for b in range(slots // 256):
            y = mm(mat[b * 256:(b + 1) * 256, :], src[...]).astype(BF)
            w = y.shape[1] // len(dsts)
            for n, dst in enumerate(dsts):
                dst[b * nb:(b + 1) * nb] = y[:, n * w:(n + 1) * w].reshape(nb, rb, w)

    def from_blocks(mat, v, write):
        v = v.reshape(slots, v.shape[-1])
        per = 256 // rows
        for b in range(slots // 256):
            y = mm(mat[b * 256:(b + 1) * 256, :], v).astype(BF)
            for n in range(per):
                write(b * per + n, y[n * rows:(n + 1) * rows])

    def a2a(n, src, dst):
        dst[t] = src[t]
        far_first(lambda s: rcopy(src.at[s], dst.at[t], a2a_send.at[n], a2a_recv.at[n], seq=s).start())

    def take(buf, sem, count):
        v = buf.at[pl.ds(0, count)]
        pltpu.make_async_copy(v, v, sem).wait()

    def whole(buf, sem):
        pltpu.make_async_copy(buf, buf, sem).wait()

    loads[2].wait()
    stack(kv_cols)
    to_blocks(put_ref, stack_ref, xkv)

    pl.semaphore_wait(barrier, n_seq - 1 + 2 * (n_dp - 1))
    a2a(0, xkv, rkv)

    loads[4].wait()
    r = iota((16, 512), 0)
    l = iota((16, 512), 1)
    j = r & 3
    pick = jnp.where(j == 0, ids_ref[0], jnp.where(j == 1, ids_ref[1], jnp.where(j == 2, ids_ref[2], ids_ref[3])))
    hit = l == pick
    block = jnp.zeros((16, CH), F32)
    for q in range(4):
        block = block + mm(one(hit & (lax.shift_right_logical(r, 2) == q)), table_ref[:, q * CH:(q + 1) * CH])

    @pl.when(my_turn)
    def _():
        k = lax.div(t, plane)
        negs_ref[carrier * per_ring + k] = block.astype(BF)
        mine = negs_ref.at[carrier * per_ring + k]

        def step(i, c):
            s = lax.rem(t + 2 * i, n_seq)
            rcopy(mine, mine, neg_send, neg_zrecv.at[k], seq=s).start()
            return c
        lax.fori_loop(1, n_seq // 2, step, 0)

    for n in range(8):
        pair_ref[n * rows:(n + 1) * rows, :head] = qkvu_ref[:, 2 * width + n * head:2 * width + (n + 1) * head]
        pair_ref[n * rows:(n + 1) * rows, head:] = qkvu_ref[:, n * head:(n + 1) * head]
    to_blocks(put_ref, pair_ref, xq, xu)
    a2a(1, xq, rq)

    i0 = iota((rows, rows), 0)
    l0 = iota((rows, rows), 1)
    send_col = jnp.sum(jnp.where(i0 == l0, send_f, 0.0), axis=1, keepdims=True)
    recv_col = jnp.sum(jnp.where(i0 == l0, recv_f, 0.0), axis=1, keepdims=True)

    def build_rows(j, c):
        l = iota((rows, slots), 1)
        i = iota((rows, slots), 0)
        slot = lax.shift_right_logical(l, 3)
        turn = (l & 7) == j
        at = pl.ds(pl.multiple_of(j * rows, rows), rows)
        get_ref[at, :] = one((recv_col == slot.astype(F32)) & turn)
        send_row = jnp.sum(jnp.where(i == slot, send_col, 0.0), axis=0, keepdims=True)
        get_back_ref[at, :] = one((send_row == i.astype(F32)) & turn)
        recv_row = jnp.concatenate([recv_f] * 8, axis=1)
        put_slot = j * (rows // 8) + lax.shift_right_logical(i, 3)
        put_back_ref[at, :] = one((recv_row == put_slot.astype(F32)) & ((i & 7) == lax.shift_right_logical(l, 7)))
        return c

    lax.fori_loop(0, 8, build_rows, 0)

    own_len = len_ref[0, t]
    len_1 = jnp.where(t >= 1, len_ref[0, lax.max(t - 1, 0)], 0)
    len_2 = jnp.where(t >= 2, len_ref[0, lax.max(t - 2, 0)], 0)
    alive = i0 < own_len
    for n, m in enumerate((alive & (l0 <= i0) & (l0 < own_len), alive & (l0 < len_1), alive & (l0 < len_2))):
        mask_ref[:, n * rows:(n + 1) * rows] = jnp.where(m, 1.0 / rows, 0.0)

    loads[3].wait()
    live_col = jnp.where(iota(coef_ref.shape, 0) < own_len, 1.0, 0.0)
    live_ref[...] = (coef_ref[...].astype(F32) * live_col).astype(BF)

    take(rkv, a2a_recv.at[0], n_seq - 1)

    def write_kv(n, y):
        kv_ref[0, :, n * CH:(n + 1) * CH] = y
    from_blocks(get_ref, rkv[...], write_kv)
    odd = lax.rem(t, 2) == 1
    even = lax.rem(t, 2) == 0

    @pl.when(t + 2 < n_seq)
    def _():
        rcopy(kv_ref.at[0], kv_ref.at[2], halo_send.at[1], halo_recv.at[1], seq=lax.rem(t + 2, n_seq)).start()

    @pl.when(even)
    def _():
        rcopy(kv_ref.at[0], kv_ref.at[1], halo_send.at[0], halo_recv.at[0], seq=mate).start()

    for lag in range(1, SPAN):
        @pl.when(t < lag)
        def _():
            kv_ref[lag] = jnp.zeros(kv_ref.shape[1:], BF)

    a2a(2, xu, ru)

    for k in range(per_ring):
        @pl.when(k * plane + carrier != t)
        def _():
            whole(negs_ref.at[carrier * per_ring + k], neg_zrecv.at[k])
    shards = negs_ref.at[pl.ds(carrier * per_ring, per_ring)]
    each_plane_peer(lambda c, where: rcopy(shards, shards, neg_xsend, neg_xrecv, **where))
    take(negs_ref, neg_xrecv, (plane - 1) * per_ring)

    n_negs = 4 * n_seq
    flat = negs_ref[...].reshape(16 * n_seq, CH)
    n = iota((n_negs, 16 * n_seq), 0)
    l = iota((n_negs, 16 * n_seq), 1)
    shard = lax.shift_right_logical(n, 2)
    ring_bits = plane.bit_length() - 1
    place = ((shard & (plane - 1)) * per_ring + lax.shift_right_logical(shard, ring_bits)) * 16 + (n & 3)
    for q in range(4):
        neg_ref[:, q * CH:(q + 1) * CH] = mm(one(l == place + 4 * q), flat).astype(BF)

    loads[5].wait()
    head_grad = mm(live_ref[...], neg_ref[...]).astype(BF)
    for b in range(width // CH):
        dmix_ref[:, b * CH:(b + 1) * CH] = mm_nt(head_grad, w_ref[b * CH:(b + 1) * CH, :])

    take(rq, a2a_recv.at[1], n_seq - 1)

    def write_q(n, y):
        q_ref[:, n * head:(n + 1) * head] = y
    from_blocks(get_ref, rq[...], write_q)

    @pl.when(t >= 2)
    def _():
        whole(kv_ref.at[2], halo_recv.at[1])

    @pl.when(odd & (t >= 2))
    def _():
        rcopy(kv_ref.at[2], kv_ref.at[1], halo_send.at[0], halo_recv.at[0], seq=mate).start()

    @pl.when(t >= 1)
    def _():
        whole(kv_ref.at[1], halo_recv.at[0])

    def lanes(h, base=0):
        return pl.ds(pl.multiple_of(base + h * head, head), head)

    def forward(h, c):
        q = q_ref[:, lanes(h)]
        k3 = kv_ref[:, :, lanes(h, width)].reshape(SPAN * rows, head)
        v3 = kv_ref[:, :, lanes(h)].reshape(SPAN * rows, head)
        s = mm_nt(q, k3) * scale
        sig = 0.5 + 0.5 * jnp.tanh(0.5 * s)
        m = mask_ref[...]
        w = (s * sig * m).astype(BF)
        wgt_ref[h] = w
        fac_ref[h] = m * scale * (sig * (1.0 + s * (1.0 - sig)))
        att_ref[:, lanes(h)] = mm(w, v3)
        return c

    lax.fori_loop(0, HEADS, forward, 0)

    step = 32
    spans = [slice(b * step, (b + 1) * step) for b in range(rows // step)]
    for at in spans:
        a = att_ref[at, :]
        cen = a - jnp.mean(a, axis=1, keepdims=True)
        inv = lax.rsqrt(jnp.mean(cen * cen, axis=1, keepdims=True) + eps)
        normed = cen * inv
        att_ref[at, :] = normed
        inv_ref[at, :] = jnp.broadcast_to(inv, (step, 128))
        du = (dmix_ref[at, :] * normed).astype(BF)
        for n in range(8):
            thin_ref[n * rows + at.start:n * rows + at.stop, :] = du[:, n * head:(n + 1) * head]
    to_blocks(put_back_ref, thin_ref, gu)
    a2a(3, gu, hu)

    take(ru, a2a_recv.at[2], n_seq - 1)

    def write_u(n, y):
        u_ref[:, n * head:(n + 1) * head] = y
    from_blocks(get_ref, ru[...], write_u)

    for at in spans:
        normed = att_ref[at, :]
        inv = inv_ref[at, :1]
        u = u_ref[at, :].astype(F32)
        mixed_ref[at, :] = (normed * u).astype(BF)
        dn = dmix_ref[at, :] * u
        da = (dn - jnp.mean(dn, axis=1, keepdims=True) - normed * jnp.mean(dn * normed, axis=1, keepdims=True)) * inv
        datt_ref[at, :] = da.astype(BF)

    def backward(h, c):
        q = q_ref[:, lanes(h)]
        k3 = kv_ref[:, :, lanes(h, width)].reshape(SPAN * rows, head)
        v3 = kv_ref[:, :, lanes(h)].reshape(SPAN * rows, head)
        da = datt_ref[:, lanes(h)]
        ds = (mm_nt(da, v3) * fac_ref[h]).astype(BF)
        thin_ref[pl.ds(pl.multiple_of(h * rows, rows), rows), :] = mm(ds, k3).astype(BF)
        kp = mm_tn(ds, q)
        vp = mm_tn(wgt_ref[h], da)
        own_ref[:, lanes(h, width)] = kp[:rows]
        own_ref[:, lanes(h)] = vp[:rows]
        for lag in range(1, SPAN):
            part_ref[lag - 1, :, lanes(h, width)] = kp[lag * rows:(lag + 1) * rows].astype(BF)
            part_ref[lag - 1, :, lanes(h)] = vp[lag * rows:(lag + 1) * rows].astype(BF)
        return c

    lax.fori_loop(0, HEADS, backward, 0)

    swap = rcopy(part_ref.at[0], back_ref.at[0], back_send.at[0], back_recv.at[0], seq=mate)
    swap.start()

    def hand_back():
        rcopy(part_ref.at[1], back_ref.at[1], back_send.at[1], back_recv.at[1], seq=lax.rem(t + n_seq - 2, n_seq)).start()

    @pl.when(even & (t >= 2))
    def _():
        hand_back()

    @pl.when(t + 2 >= n_seq)
    def _():
        back_ref[1] = jnp.zeros(back_ref.shape[1:], BF)

    per_block = rows // d_rows
    for b in range(width // rows):
        y = mm_tn(mixed_ref[:, b * rows:(b + 1) * rows], live_ref[...])
        for n in range(per_block):
            s = b * per_block + n
            sum_x[s % plane * per_ring + s // plane] = y[n * d_rows:(n + 1) * d_rows]
    own_at = pl.ds(carrier * per_ring, per_ring)
    sum_r[own_at] = sum_x[own_at]
    each_plane_peer(lambda c, where: rcopy(sum_x.at[pl.ds(c * per_ring, per_ring)], sum_r.at[own_at], sx_send, sx_recv, **where))

    whole(back_ref.at[0], back_recv.at[0])

    @pl.when(odd & (t >= 2))
    def _():
        part_ref[1] = (part_ref[1].astype(F32) + back_ref[0].astype(F32)).astype(BF)
        hand_back()

    to_blocks(put_back_ref, thin_ref, gq)
    a2a(4, gq, hq)

    take(sum_r, sx_recv, (plane - 1) * per_ring)
    chip = lax.div(t, 2)
    for k in range(per_ring):
        s = k * plane + carrier
        sum_z[k] = lax.fori_loop(1, plane, lambda i, acc: acc + sum_r[i * per_ring + k], sum_r[k]).astype(BF)

        @pl.when(s != t)
        def _():
            rcopy(sum_z.at[k], sum_zr.at[chip], sz_send.at[k], sz_recv, seq=s).start()

        @pl.when(s == t)
        def _():
            sum_zr[chip] = sum_z[k]

    @pl.when(t + 2 < n_seq)
    def _():
        whole(back_ref.at[1], back_recv.at[1])
    keep = jnp.where(even, 1.0, 0.0)
    for n in range(8):
        c = slice(n * CH, (n + 1) * CH)
        y = own_ref[:, c] + back_ref[0, :, c].astype(F32) * keep + back_ref[1, :, c].astype(F32)
        stack_ref[n * rows:(n + 1) * rows, :] = y.astype(BF)
    to_blocks(put_back_ref, stack_ref, gkv)
    a2a(5, gkv, hkv)

    for b in range(width // CH):
        out_ref[:, b * CH:(b + 1) * CH] = mm(mixed_ref[...], w_ref[:, b * CH:(b + 1) * CH]).astype(BF)

    @pl.when(my_turn)
    def _():
        take(sum_zr, sz_recv, n_seq // 2 - 1)
        sum_f[...] = lax.fori_loop(1, n_seq // 2, lambda i, acc: acc + sum_zr[i].astype(F32), sum_zr[0].astype(F32))
        each_dp_peer(lambda d: rcopy(sum_f, sum_f, sf_send, sf_recv, dp=d).start())

    @pl.when(jnp.logical_not(my_turn))
    def _():
        whole(sum_f, sf_recv)

    total = sum_f[...]
    top = total.astype(BF)
    low = (total - top.astype(F32)).astype(BF)
    cols = width // n_dp
    if cols >= 128:
        nb = neg_ref[:, pl.ds(pl.multiple_of(g * cols, cols), cols)]
        dw_ref[...] = mm(top, nb) + mm(low, nb)
    else:
        per = 128 // cols
        nb = neg_ref[:, pl.ds(pl.multiple_of(lax.div(g, per) * 128, 128), 128)]
        y = mm(top, nb) + mm(low, nb)
        z = y[:, :cols]
        for n in range(1, per):
            z = jnp.where(lax.rem(g, per) == n, y[:, n * cols:(n + 1) * cols], z)
        dw_ref[...] = z

    take(hu, a2a_recv.at[3], n_seq - 1)
    take(hq, a2a_recv.at[4], n_seq - 1)

    def home_uq(n, y):
        home_ref[:, n * head:(n + 1) * head] = y[:, :head]
        home_ref[:, 2 * width + n * head:2 * width + (n + 1) * head] = y[:, head:]
    both = jnp.concatenate([hu[...].reshape(slots, head), hq[...].reshape(slots, head)], axis=1)
    from_blocks(get_back_ref, both, home_uq)

    for n, buf in enumerate((xkv, xq, xu, gu, gq)):
        take(buf, a2a_send.at[n], n_seq - 1)
    take(negs_ref, neg_xsend, (plane - 1) * per_ring)
    take(sum_x, sx_send, (plane - 1) * per_ring)

    @pl.when(my_turn)
    def _():
        take(negs_ref, neg_send, n_seq // 2 - 1)
        take(sum_r, sf_send, n_dp - 1)

    for k in range(per_ring):
        @pl.when(k * plane + carrier != t)
        def _():
            whole(sum_z.at[k], sz_send.at[k])

    @pl.when(t + 2 < n_seq)
    def _():
        whole(kv_ref.at[0], halo_send.at[1])

    @pl.when(even | (t >= 2))
    def _():
        whole(kv_ref.at[0], halo_send.at[0])
    whole(part_ref.at[0], back_send.at[0])

    @pl.when(t >= 2)
    def _():
        whole(part_ref.at[1], back_send.at[1])

    take(hkv, a2a_recv.at[5], n_seq - 1)

    def home_kv(n, y):
        home_ref[:, kv_cols[n]:kv_cols[n] + CH] = y
    from_blocks(get_back_ref, hkv[...], home_kv)
    take(gkv, a2a_send.at[5], n_seq - 1)


def put_out(a, b, c, out_a, out_b, out_c, sem):
    copies = [pltpu.make_async_copy(x, y, sem.at[n]) for n, (x, y) in enumerate(((a, out_a), (b, out_b), (c, out_c)))]
    for copy in copies:
        copy.start()
    for copy in copies:
        copy.wait()


def on_device(n_dp, n_seq, qkvu, w_out, head_coef, item_table, neg_ids, send_order, recv_order, tile_len):
    rows = qkvu.shape[0]
    width = w_out.shape[0]
    slots = 8 * rows
    rb = slots // n_seq
    per_ring = n_seq // (2 * n_dp)
    d_rows = width // n_seq
    negs = head_coef.shape[1]
    vm = pl.BlockSpec(memory_space=pltpu.VMEM)
    sm = pl.BlockSpec(memory_space=pltpu.SMEM)
    dma = pltpu.SemaphoreType.DMA
    any_space = pl.BlockSpec(memory_space=pl.ANY)
    wide = pltpu.VMEM((n_seq, rb, CH), BF)
    thin = pltpu.VMEM((n_seq, rb, CH // 2), BF)
    square = pltpu.VMEM((slots, slots), BF)
    results = pl.pallas_call(
        functools.partial(kernel, n_dp, n_seq),
        out_shape=(
            pltpu.VMEM((rows, width), BF),
            pltpu.VMEM((rows, 4 * width), BF),
            pltpu.VMEM((d_rows, width // n_dp), F32),
        ),
        in_specs=[sm, sm] + [any_space] * 6,
        out_specs=(vm, vm, vm),
        scratch_shapes=[
            pltpu.VMEM(send_order.shape, jnp.int32), pltpu.VMEM(recv_order.shape, jnp.int32),
            pltpu.VMEM(qkvu.shape, BF), pltpu.VMEM(head_coef.shape, BF),
            pltpu.VMEM(item_table.shape, BF), pltpu.VMEM(w_out.shape, BF),
            square, square, square, square,
            pltpu.VMEM((slots, CH), BF), pltpu.VMEM((slots, CH), BF), pltpu.VMEM((slots, CH // 2), BF),
            wide, wide, wide, wide,
            thin, thin, thin, thin, thin, thin, thin, thin,
            pltpu.VMEM((SPAN, rows, 2 * width), BF),
            pltpu.VMEM((rows, width), BF),
            pltpu.VMEM((rows, width), BF),
            pltpu.VMEM((rows, 2 * width), F32),
            pltpu.VMEM((SPAN - 1, rows, 2 * width), BF),
            pltpu.VMEM((SPAN - 1, rows, 2 * width), BF),
            pltpu.VMEM((HEADS, rows, SPAN * rows), BF),
            pltpu.VMEM((HEADS, rows, SPAN * rows), F32),
            pltpu.VMEM((rows, SPAN * rows), F32),
            pltpu.VMEM((rows, width), F32),
            pltpu.VMEM((rows, 128), F32),
            pltpu.VMEM((rows, width), BF),
            pltpu.VMEM((rows, width), BF),
            pltpu.VMEM((rows, negs), BF),
            pltpu.VMEM((rows, width), F32),
            pltpu.VMEM((n_seq, 16, CH), BF),
            pltpu.VMEM((negs, width), BF),
            pltpu.VMEM((n_seq, d_rows, negs), F32),
            pltpu.VMEM((n_seq, d_rows, negs), F32),
            pltpu.VMEM((per_ring, d_rows, negs), BF),
            pltpu.VMEM((n_seq // 2, d_rows, negs), BF),
            pltpu.VMEM((d_rows, negs), F32),
            dma((6,)), dma((6,)), dma((6,)), dma, dma((per_ring,)), dma, dma,
            dma((SPAN - 1,)), dma((SPAN - 1,)), dma((SPAN - 1,)), dma((SPAN - 1,)),
            dma, dma, dma((per_ring,)), dma, dma, dma,
        ],
        compiler_params=pltpu.CompilerParams(
            collective_id=0, has_side_effects=True, vmem_limit_bytes=60 * 2**20
        ),
    )(neg_ids, tile_len, qkvu, head_coef, send_order, recv_order, w_out, item_table)
    return pl.pallas_call(
        put_out,
        out_shape=tuple(jax.ShapeDtypeStruct(r.shape, r.dtype) for r in results),
        in_specs=[pl.BlockSpec(memory_space=pltpu.VMEM)] * 3,
        out_specs=(any_space,) * 3,
        scratch_shapes=[dma((3,))],
        compiler_params=pltpu.CompilerParams(vmem_limit_bytes=4 * 2**20),
    )(*results)


def solution(mesh):
    placed = (
        P(("dp", "seq"), None),
        P(),
        P(("dp", "seq"), None),
        P("seq", None),
        P("seq"),
        P(("dp", "seq"), None),
        P(("dp", "seq"), None),
        P("dp", None),
    )
    return jax.shard_map(
        functools.partial(on_device, mesh.shape["dp"], mesh.shape["seq"]),
        mesh=mesh,
        in_specs=placed,
        out_specs=(P(("dp", "seq"), None), P(("dp", "seq"), None), P("seq", "dp")),
        check_vma=False,
    )
```

```python
import functools
import math

import jax
import jax.numpy as jnp
from jax import lax
from jax.experimental import pallas as pl
from jax.experimental.pallas import tpu as pltpu
from jax.sharding import PartitionSpec as P

HEADS = 8
SPAN = 3
CH = 256
eps = 1e-05
BF = jnp.bfloat16
F32 = jnp.float32
MESH = pl.DeviceIdType.MESH


def iota(shape, dim):
    return lax.broadcasted_iota(jnp.int32, shape, dim)


def mm(a, b):
    return jnp.dot(a, b, preferred_element_type=F32)


def mm_nt(a, b):
    return lax.dot_general(a, b, (((1,), (1,)), ((), ())), preferred_element_type=F32)


def mm_tn(a, b):
    return lax.dot_general(a, b, (((0,), (0,)), ((), ())), preferred_element_type=F32)


def kernel(
    n_dp, n_seq,
    ids_ref, len_ref, qkvu_ref, coef_ref, send_ref, recv_ref, w_hbm, table_hbm,
    out_ref, home_ref, dw_ref,
    w_ref, table_ref,
    put_ref, get_ref, put_back_ref, get_back_ref, stack_ref, pair_ref, thin_ref,
    xkv, rkv, gkv, hkv,
    xq, xu, rq, ru, gq, gu, hq, hu,
    kv_ref, q_ref, u_ref, own_ref, part_ref, back_ref,
    wgt_ref, fac_ref, mask_ref, att_ref, inv_ref, datt_ref, mixed_ref, live_ref, dmix_ref,
    negs_ref, neg_ref, sum_x, sum_r, sum_z, sum_zr, sum_f,
    load_sem, a2a_send, a2a_recv, neg_send, neg_zrecv, neg_xsend, neg_xrecv,
    halo_send, halo_recv, back_send, back_recv,
    sx_send, sx_recv, sz_send, sz_recv, sf_send, sf_recv,
):
    g = lax.axis_index("dp")
    t = lax.axis_index("seq")
    rows, width = att_ref.shape
    slots = 8 * rows
    head = width // HEADS
    scale = 1.0 / math.sqrt(head)
    per_ring = n_seq // n_dp
    d_rows = width // n_seq
    rb = slots // n_seq
    my_turn = lax.rem(t, n_dp) == g

    def rcopy(src, dst, ssem, rsem, **where):
        return pltpu.make_async_remote_copy(
            src_ref=src, dst_ref=dst, send_sem=ssem, recv_sem=rsem,
            device_id=where, device_id_type=MESH,
        )

    def each_seq_peer(body):
        def step(i, c):
            body(lax.rem(t + i, n_seq))
            return c
        lax.fori_loop(1, n_seq, step, 0)

    def far_first(body):
        half = n_seq // 2

        def step(i, c):
            k = half - i
            body(lax.rem(t + k, n_seq))

            @pl.when(k < half)
            def _():
                body(lax.rem(t + n_seq - k, n_seq))
            return c
        lax.fori_loop(0, half, step, 0)

    def each_dp_peer(body):
        def step(i, c):
            body(lax.rem(g + i, n_dp))
            return c
        lax.fori_loop(1, n_dp, step, 0)

    barrier = pltpu.get_barrier_semaphore()
    each_seq_peer(lambda s: pl.semaphore_signal(barrier, inc=1, device_id={"seq": s}, device_id_type=MESH))
    each_dp_peer(lambda d: pl.semaphore_signal(barrier, inc=1, device_id={"dp": d}, device_id_type=MESH))

    load_table = pltpu.make_async_copy(table_hbm, table_ref, load_sem.at[0])
    load_w = pltpu.make_async_copy(w_hbm, w_ref, load_sem.at[1])
    load_table.start()
    load_w.start()

    send_f = send_ref[...].astype(F32)
    recv_f = recv_ref[...].astype(F32)
    one = lambda m: jnp.where(m, 1.0, 0.0).astype(BF)

    def build_put(b, c):
        i0 = iota((rows, rows), 0)
        l0 = iota((rows, rows), 1)
        slot = b * (rows // 8) + lax.shift_right_logical(i0, 3)
        idx = jnp.sum(jnp.where(l0 == slot, send_f, 0.0), axis=1, keepdims=True)
        i = iota((rows, slots), 0)
        l = iota((rows, slots), 1)
        m = (idx == (l & (rows - 1)).astype(F32)) & ((i & 7) == lax.shift_right_logical(l, 7))
        put_ref[pl.ds(pl.multiple_of(b * rows, rows), rows), :] = one(m)
        return c

    lax.fori_loop(0, 8, build_put, 0)

    def stack(starts):
        for n, c in enumerate(starts):
            stack_ref[n * rows:(n + 1) * rows, :] = qkvu_ref[:, c:c + CH]

    kv_cols = [width + n * CH for n in range(4)] + [3 * width + n * CH for n in range(4)]

    def to_blocks(mat, src, *dsts):
        nb = 256 // rb
        for b in range(slots // 256):
            y = mm(mat[b * 256:(b + 1) * 256, :], src[...]).astype(BF)
            w = y.shape[1] // len(dsts)
            for n, dst in enumerate(dsts):
                dst[b * nb:(b + 1) * nb] = y[:, n * w:(n + 1) * w].reshape(nb, rb, w)

    def from_blocks(mat, v, write):
        v = v.reshape(slots, v.shape[-1])
        per = 256 // rows
        for b in range(slots // 256):
            y = mm(mat[b * 256:(b + 1) * 256, :], v).astype(BF)
            for n in range(per):
                write(b * per + n, y[n * rows:(n + 1) * rows])

    def a2a(n, src, dst):
        dst[t] = src[t]
        far_first(lambda s: rcopy(src.at[s], dst.at[t], a2a_send.at[n], a2a_recv.at[n], seq=s).start())

    def take(buf, sem, count):
        v = buf.at[pl.ds(0, count)]
        pltpu.make_async_copy(v, v, sem).wait()

    def whole(buf, sem):
        pltpu.make_async_copy(buf, buf, sem).wait()

    stack(kv_cols)
    to_blocks(put_ref, stack_ref, xkv)

    pl.semaphore_wait(barrier, n_seq - 1 + n_dp - 1)
    a2a(0, xkv, rkv)

    load_table.wait()
    r = iota((16, 512), 0)
    l = iota((16, 512), 1)
    j = r & 3
    pick = jnp.where(j == 0, ids_ref[0], jnp.where(j == 1, ids_ref[1], jnp.where(j == 2, ids_ref[2], ids_ref[3])))
    hit = l == pick
    block = jnp.zeros((16, CH), F32)
    for q in range(4):
        block = block + mm(one(hit & (lax.shift_right_logical(r, 2) == q)), table_ref[:, q * CH:(q + 1) * CH])

    @pl.when(my_turn)
    def _():
        negs_ref[g * per_ring + lax.div(t, n_dp)] = block.astype(BF)
        mine = negs_ref.at[g * per_ring + lax.div(t, n_dp)]
        far_first(lambda s: rcopy(mine, mine, neg_send, neg_zrecv.at[lax.div(t, n_dp)], seq=s).start())

    for n in range(8):
        pair_ref[n * rows:(n + 1) * rows, :head] = qkvu_ref[:, 2 * width + n * head:2 * width + (n + 1) * head]
        pair_ref[n * rows:(n + 1) * rows, head:] = qkvu_ref[:, n * head:(n + 1) * head]
    to_blocks(put_ref, pair_ref, xq, xu)
    a2a(1, xq, rq)

    i0 = iota((rows, rows), 0)
    l0 = iota((rows, rows), 1)
    send_col = jnp.sum(jnp.where(i0 == l0, send_f, 0.0), axis=1, keepdims=True)
    recv_col = jnp.sum(jnp.where(i0 == l0, recv_f, 0.0), axis=1, keepdims=True)

    def build_rows(j, c):
        l = iota((rows, slots), 1)
        i = iota((rows, slots), 0)
        slot = lax.shift_right_logical(l, 3)
        turn = (l & 7) == j
        at = pl.ds(pl.multiple_of(j * rows, rows), rows)
        get_ref[at, :] = one((recv_col == slot.astype(F32)) & turn)
        send_row = jnp.sum(jnp.where(i == slot, send_col, 0.0), axis=0, keepdims=True)
        get_back_ref[at, :] = one((send_row == i.astype(F32)) & turn)
        recv_row = jnp.concatenate([recv_f] * 8, axis=1)
        put_slot = j * (rows // 8) + lax.shift_right_logical(i, 3)
        put_back_ref[at, :] = one((recv_row == put_slot.astype(F32)) & ((i & 7) == lax.shift_right_logical(l, 7)))
        return c

    lax.fori_loop(0, 8, build_rows, 0)

    own_len = len_ref[0, t]
    len_1 = jnp.where(t >= 1, len_ref[0, lax.max(t - 1, 0)], 0)
    len_2 = jnp.where(t >= 2, len_ref[0, lax.max(t - 2, 0)], 0)
    alive = i0 < own_len
    for n, m in enumerate((alive & (l0 <= i0) & (l0 < own_len), alive & (l0 < len_1), alive & (l0 < len_2))):
        mask_ref[:, n * rows:(n + 1) * rows] = jnp.where(m, 1.0 / rows, 0.0)

    live_col = jnp.where(iota(coef_ref.shape, 0) < own_len, 1.0, 0.0)
    live_ref[...] = (coef_ref[...].astype(F32) * live_col).astype(BF)

    take(rkv, a2a_recv.at[0], n_seq - 1)

    def write_kv(n, y):
        kv_ref[0, :, n * CH:(n + 1) * CH] = y
    from_blocks(get_ref, rkv[...], write_kv)
    odd = lax.rem(t, 2) == 1
    even = lax.rem(t, 2) == 0
    mate = t + 1 - 2 * lax.rem(t, 2)

    @pl.when(t + 2 < n_seq)
    def _():
        rcopy(kv_ref.at[0], kv_ref.at[2], halo_send.at[1], halo_recv.at[1], seq=lax.rem(t + 2, n_seq)).start()

    @pl.when(even)
    def _():
        rcopy(kv_ref.at[0], kv_ref.at[1], halo_send.at[0], halo_recv.at[0], seq=mate).start()

    for lag in range(1, SPAN):
        @pl.when(t < lag)
        def _():
            kv_ref[lag] = jnp.zeros(kv_ref.shape[1:], BF)

    a2a(2, xu, ru)

    for k in range(per_ring):
        @pl.when(k * n_dp + g != t)
        def _():
            whole(negs_ref.at[g * per_ring + k], neg_zrecv.at[k])
    shards = negs_ref.at[pl.ds(g * per_ring, per_ring)]
    each_dp_peer(lambda d: rcopy(shards, shards, neg_xsend, neg_xrecv, dp=d).start())
    take(negs_ref, neg_xrecv, (n_dp - 1) * per_ring)

    n_negs = 4 * n_seq
    flat = negs_ref[...].reshape(16 * n_seq, CH)
    n = iota((n_negs, 16 * n_seq), 0)
    l = iota((n_negs, 16 * n_seq), 1)
    shard = lax.shift_right_logical(n, 2)
    ring_bits = n_dp.bit_length() - 1
    place = ((shard & (n_dp - 1)) * per_ring + lax.shift_right_logical(shard, ring_bits)) * 16 + (n & 3)
    for q in range(4):
        neg_ref[:, q * CH:(q + 1) * CH] = mm(one(l == place + 4 * q), flat).astype(BF)

    load_w.wait()
    head_grad = mm(live_ref[...], neg_ref[...]).astype(BF)
    for b in range(width // CH):
        dmix_ref[:, b * CH:(b + 1) * CH] = mm_nt(head_grad, w_ref[b * CH:(b + 1) * CH, :])

    take(rq, a2a_recv.at[1], n_seq - 1)

    def write_q(n, y):
        q_ref[:, n * head:(n + 1) * head] = y
    from_blocks(get_ref, rq[...], write_q)

    @pl.when(t >= 2)
    def _():
        whole(kv_ref.at[2], halo_recv.at[1])

    @pl.when(odd & (t >= 2))
    def _():
        rcopy(kv_ref.at[2], kv_ref.at[1], halo_send.at[0], halo_recv.at[0], seq=mate).start()

    @pl.when(t >= 1)
    def _():
        whole(kv_ref.at[1], halo_recv.at[0])

    def lanes(h, base=0):
        return pl.ds(pl.multiple_of(base + h * head, head), head)

    def forward(h, c):
        q = q_ref[:, lanes(h)]
        k3 = kv_ref[:, :, lanes(h, width)].reshape(SPAN * rows, head)
        v3 = kv_ref[:, :, lanes(h)].reshape(SPAN * rows, head)
        s = mm_nt(q, k3) * scale
        sig = 0.5 + 0.5 * jnp.tanh(0.5 * s)
        m = mask_ref[...]
        w = (s * sig * m).astype(BF)
        wgt_ref[h] = w
        fac_ref[h] = m * scale * (sig * (1.0 + s * (1.0 - sig)))
        att_ref[:, lanes(h)] = mm(w, v3)
        return c

    lax.fori_loop(0, HEADS, forward, 0)

    step = 32
    spans = [slice(b * step, (b + 1) * step) for b in range(rows // step)]
    for at in spans:
        a = att_ref[at, :]
        cen = a - jnp.mean(a, axis=1, keepdims=True)
        inv = lax.rsqrt(jnp.mean(cen * cen, axis=1, keepdims=True) + eps)
        normed = cen * inv
        att_ref[at, :] = normed
        inv_ref[at, :] = jnp.broadcast_to(inv, (step, 128))
        du = (dmix_ref[at, :] * normed).astype(BF)
        for n in range(8):
            thin_ref[n * rows + at.start:n * rows + at.stop, :] = du[:, n * head:(n + 1) * head]
    to_blocks(put_back_ref, thin_ref, gu)
    a2a(3, gu, hu)

    take(ru, a2a_recv.at[2], n_seq - 1)

    def write_u(n, y):
        u_ref[:, n * head:(n + 1) * head] = y
    from_blocks(get_ref, ru[...], write_u)

    for at in spans:
        normed = att_ref[at, :]
        inv = inv_ref[at, :1]
        u = u_ref[at, :].astype(F32)
        mixed_ref[at, :] = (normed * u).astype(BF)
        dn = dmix_ref[at, :] * u
        da = (dn - jnp.mean(dn, axis=1, keepdims=True) - normed * jnp.mean(dn * normed, axis=1, keepdims=True)) * inv
        datt_ref[at, :] = da.astype(BF)

    def backward(h, c):
        q = q_ref[:, lanes(h)]
        k3 = kv_ref[:, :, lanes(h, width)].reshape(SPAN * rows, head)
        v3 = kv_ref[:, :, lanes(h)].reshape(SPAN * rows, head)
        da = datt_ref[:, lanes(h)]
        ds = (mm_nt(da, v3) * fac_ref[h]).astype(BF)
        thin_ref[pl.ds(pl.multiple_of(h * rows, rows), rows), :] = mm(ds, k3).astype(BF)
        kp = mm_tn(ds, q)
        vp = mm_tn(wgt_ref[h], da)
        own_ref[:, lanes(h, width)] = kp[:rows]
        own_ref[:, lanes(h)] = vp[:rows]
        for lag in range(1, SPAN):
            part_ref[lag - 1, :, lanes(h, width)] = kp[lag * rows:(lag + 1) * rows].astype(BF)
            part_ref[lag - 1, :, lanes(h)] = vp[lag * rows:(lag + 1) * rows].astype(BF)
        return c

    lax.fori_loop(0, HEADS, backward, 0)

    swap = rcopy(part_ref.at[0], back_ref.at[0], back_send.at[0], back_recv.at[0], seq=mate)
    swap.start()

    def hand_back():
        rcopy(part_ref.at[1], back_ref.at[1], back_send.at[1], back_recv.at[1], seq=lax.rem(t + n_seq - 2, n_seq)).start()

    @pl.when(even & (t >= 2))
    def _():
        hand_back()

    @pl.when(t + 2 >= n_seq)
    def _():
        back_ref[1] = jnp.zeros(back_ref.shape[1:], BF)

    per_block = rows // d_rows
    for b in range(width // rows):
        y = mm_tn(mixed_ref[:, b * rows:(b + 1) * rows], live_ref[...])
        for n in range(per_block):
            s = b * per_block + n
            sum_x[s % n_dp, s // n_dp] = y[n * d_rows:(n + 1) * d_rows]
    sum_r[g] = sum_x[g]
    each_dp_peer(lambda d: rcopy(sum_x.at[d], sum_r.at[g], sx_send, sx_recv, dp=d).start())

    whole(back_ref.at[0], back_recv.at[0])

    @pl.when(odd & (t >= 2))
    def _():
        part_ref[1] = (part_ref[1].astype(F32) + back_ref[0].astype(F32)).astype(BF)
        hand_back()

    to_blocks(put_back_ref, thin_ref, gq)
    a2a(4, gq, hq)

    take(sum_r, sx_recv, n_dp - 1)
    sum_z[...] = lax.fori_loop(1, n_dp, lambda i, acc: acc + sum_r[i], sum_r[0]).astype(BF)
    for k in range(per_ring):
        s = k * n_dp + g

        @pl.when(s != t)
        def _():
            rcopy(sum_z.at[k], sum_zr.at[t], sz_send.at[k], sz_recv, seq=s).start()

        @pl.when(s == t)
        def _():
            sum_zr[t] = sum_z[k]

    @pl.when(t + 2 < n_seq)
    def _():
        whole(back_ref.at[1], back_recv.at[1])
    keep = jnp.where(even, 1.0, 0.0)
    for n in range(8):
        c = slice(n * CH, (n + 1) * CH)
        y = own_ref[:, c] + back_ref[0, :, c].astype(F32) * keep + back_ref[1, :, c].astype(F32)
        stack_ref[n * rows:(n + 1) * rows, :] = y.astype(BF)
    to_blocks(put_back_ref, stack_ref, gkv)
    a2a(5, gkv, hkv)

    for b in range(width // CH):
        out_ref[:, b * CH:(b + 1) * CH] = mm(mixed_ref[...], w_ref[:, b * CH:(b + 1) * CH]).astype(BF)

    @pl.when(my_turn)
    def _():
        take(sum_zr, sz_recv, n_seq - 1)
        sum_f[...] = lax.fori_loop(1, n_seq, lambda i, acc: acc + sum_zr[i].astype(F32), sum_zr[0].astype(F32))
        each_dp_peer(lambda d: rcopy(sum_f, sum_f, sf_send.at[d], sf_recv, dp=d).start())

    @pl.when(jnp.logical_not(my_turn))
    def _():
        whole(sum_f, sf_recv)

    total = sum_f[...]
    top = total.astype(BF)
    low = (total - top.astype(F32)).astype(BF)
    cols = width // n_dp
    if cols >= 128:
        nb = neg_ref[:, pl.ds(pl.multiple_of(g * cols, cols), cols)]
        dw_ref[...] = mm(top, nb) + mm(low, nb)
    else:
        per = 128 // cols
        nb = neg_ref[:, pl.ds(pl.multiple_of(lax.div(g, per) * 128, 128), 128)]
        y = mm(top, nb) + mm(low, nb)
        z = y[:, :cols]
        for n in range(1, per):
            z = jnp.where(lax.rem(g, per) == n, y[:, n * cols:(n + 1) * cols], z)
        dw_ref[...] = z

    take(hu, a2a_recv.at[3], n_seq - 1)
    take(hq, a2a_recv.at[4], n_seq - 1)

    def home_uq(n, y):
        home_ref[:, n * head:(n + 1) * head] = y[:, :head]
        home_ref[:, 2 * width + n * head:2 * width + (n + 1) * head] = y[:, head:]
    both = jnp.concatenate([hu[...].reshape(slots, head), hq[...].reshape(slots, head)], axis=1)
    from_blocks(get_back_ref, both, home_uq)

    for n, buf in enumerate((xkv, xq, xu, gu, gq)):
        take(buf, a2a_send.at[n], n_seq - 1)
    take(negs_ref, neg_xsend, (n_dp - 1) * per_ring)
    take(sum_x, sx_send, n_dp - 1)

    @pl.when(my_turn)
    def _():
        take(negs_ref, neg_send, n_seq - 1)
        each_dp_peer(lambda d: whole(sum_f, sf_send.at[d]))

    for k in range(per_ring):
        @pl.when(k * n_dp + g != t)
        def _():
            whole(sum_z.at[k], sz_send.at[k])

    @pl.when(t + 2 < n_seq)
    def _():
        whole(kv_ref.at[0], halo_send.at[1])

    @pl.when(even | (t >= 2))
    def _():
        whole(kv_ref.at[0], halo_send.at[0])
    whole(part_ref.at[0], back_send.at[0])

    @pl.when(t >= 2)
    def _():
        whole(part_ref.at[1], back_send.at[1])

    take(hkv, a2a_recv.at[5], n_seq - 1)

    def home_kv(n, y):
        home_ref[:, kv_cols[n]:kv_cols[n] + CH] = y
    from_blocks(get_back_ref, hkv[...], home_kv)
    take(gkv, a2a_send.at[5], n_seq - 1)


def put_out(a, b, c, out_a, out_b, out_c, sem):
    copies = [pltpu.make_async_copy(x, y, sem.at[n]) for n, (x, y) in enumerate(((a, out_a), (b, out_b), (c, out_c)))]
    for copy in copies:
        copy.start()
    for copy in copies:
        copy.wait()


def on_device(n_dp, n_seq, qkvu, w_out, head_coef, item_table, neg_ids, send_order, recv_order, tile_len):
    rows = qkvu.shape[0]
    width = w_out.shape[0]
    slots = 8 * rows
    rb = slots // n_seq
    per_ring = n_seq // n_dp
    d_rows = width // n_seq
    negs = head_coef.shape[1]
    vm = pl.BlockSpec(memory_space=pltpu.VMEM)
    sm = pl.BlockSpec(memory_space=pltpu.SMEM)
    dma = pltpu.SemaphoreType.DMA
    any_space = pl.BlockSpec(memory_space=pl.ANY)
    wide = pltpu.VMEM((n_seq, rb, CH), BF)
    thin = pltpu.VMEM((n_seq, rb, CH // 2), BF)
    square = pltpu.VMEM((slots, slots), BF)
    results = pl.pallas_call(
        functools.partial(kernel, n_dp, n_seq),
        out_shape=(
            pltpu.VMEM((rows, width), BF),
            pltpu.VMEM((rows, 4 * width), BF),
            pltpu.VMEM((d_rows, width // n_dp), F32),
        ),
        in_specs=[sm, sm, vm, vm, vm, vm, any_space, any_space],
        out_specs=(vm, vm, vm),
        scratch_shapes=[
            pltpu.VMEM(w_out.shape, BF), pltpu.VMEM(item_table.shape, BF),
            square, square, square, square,
            pltpu.VMEM((slots, CH), BF), pltpu.VMEM((slots, CH), BF), pltpu.VMEM((slots, CH // 2), BF),
            wide, wide, wide, wide,
            thin, thin, thin, thin, thin, thin, thin, thin,
            pltpu.VMEM((SPAN, rows, 2 * width), BF),
            pltpu.VMEM((rows, width), BF),
            pltpu.VMEM((rows, width), BF),
            pltpu.VMEM((rows, 2 * width), F32),
            pltpu.VMEM((SPAN - 1, rows, 2 * width), BF),
            pltpu.VMEM((SPAN - 1, rows, 2 * width), BF),
            pltpu.VMEM((HEADS, rows, SPAN * rows), BF),
            pltpu.VMEM((HEADS, rows, SPAN * rows), F32),
            pltpu.VMEM((rows, SPAN * rows), F32),
            pltpu.VMEM((rows, width), F32),
            pltpu.VMEM((rows, 128), F32),
            pltpu.VMEM((rows, width), BF),
            pltpu.VMEM((rows, width), BF),
            pltpu.VMEM((rows, negs), BF),
            pltpu.VMEM((rows, width), F32),
            pltpu.VMEM((n_seq, 16, CH), BF),
            pltpu.VMEM((negs, width), BF),
            pltpu.VMEM((n_dp, per_ring, d_rows, negs), F32),
            pltpu.VMEM((n_dp, per_ring, d_rows, negs), F32),
            pltpu.VMEM((per_ring, d_rows, negs), BF),
            pltpu.VMEM((n_seq, d_rows, negs), BF),
            pltpu.VMEM((d_rows, negs), F32),
            dma((2,)), dma((6,)), dma((6,)), dma, dma((per_ring,)), dma, dma,
            dma((SPAN - 1,)), dma((SPAN - 1,)), dma((SPAN - 1,)), dma((SPAN - 1,)),
            dma, dma, dma((per_ring,)), dma, dma((n_dp,)), dma,
        ],
        compiler_params=pltpu.CompilerParams(
            collective_id=0, has_side_effects=True, vmem_limit_bytes=60 * 2**20
        ),
    )(neg_ids, tile_len, qkvu, head_coef, send_order, recv_order, w_out, item_table)
    return pl.pallas_call(
        put_out,
        out_shape=tuple(jax.ShapeDtypeStruct(r.shape, r.dtype) for r in results),
        in_specs=[vm] * 3,
        out_specs=(any_space,) * 3,
        scratch_shapes=[dma((3,))],
        compiler_params=pltpu.CompilerParams(vmem_limit_bytes=4 * 2**20),
    )(*results)


def solution(mesh):
    placed = (
        P(("dp", "seq"), None),
        P(),
        P(("dp", "seq"), None),
        P("seq", None),
        P("seq"),
        P(("dp", "seq"), None),
        P(("dp", "seq"), None),
        P("dp", None),
    )
    return jax.shard_map(
        functools.partial(on_device, mesh.shape["dp"], mesh.shape["seq"]),
        mesh=mesh,
        in_specs=placed,
        out_specs=(P(("dp", "seq"), None), P(("dp", "seq"), None), P("seq", "dp")),
        check_vma=False,
    )
```
